32 devices in a mesh: seq: 2 (over core), batch: 16 (over z, y, x).
Axes of the slice: x: 2, y: 2, z: 4, core: 2. Of those that a mesh axis runs over, the one named last changes fastest.
Arguments:
- tokens: bfloat16 [32, 1024, 768], P('batch', 'seq'), may hold values from -6 to 6
- grad_out: bfloat16 [32, 1024, 768], P('batch', 'seq'), may hold values from -6 to 6
- lengths: int32 [32], P('batch'), may hold values from 64 to 1024, as said below
- owners: int32 [288], replicated, may hold values from 0 to 31, as said below
- weight_slots: float32 [320, 32, 768], P(('seq', 'batch')), may hold values from -1 to 1
- first_slots: float32 [320, 32, 768], P(('seq', 'batch')), may hold values from -48.223551 to 48.223551
- second_slots: float32 [320, 32, 768], P(('seq', 'batch')), may hold values from 0.16384 to 94.37184
- small_params: float32 [12, 768], replicated, may hold values from -0.4 to 1.4
- small_first: float32 [12, 768], replicated, may hold values from -96 to 96
- small_second: float32 [12, 768], replicated, may hold values from 9.8304 to 163.84
- step_count: int32 [1], replicated, may hold values from 2 to 7
Outputs:
- layer_out: bfloat16 [32, 1024, 768], P('batch', 'seq')
- grad_in: float32 [32, 1024, 768], P('batch', 'seq')
- grad_slots: float32 [320, 32, 768], P(('seq', 'batch'))
- new_slots: float32 [320, 32, 768], P(('seq', 'batch'))
- new_first_slots: float32 [320, 32, 768], P(('seq', 'batch'))
- new_second_slots: float32 [320, 32, 768], P(('seq', 'batch'))
- small_grad: float32 [12, 768], replicated
- new_small: float32 [12, 768], replicated
- new_small_first: float32 [12, 768], replicated
- new_small_second: float32 [12, 768], replicated
The draws below stay inside these ranges and needn't reach their ends.
Inputs may be any that keep to these rules, and one draw needn't show every extreme that they name: `lengths`: positions at or after a sequence's length are padding; some sequence has exactly 1024 live tokens and some exactly 64. `owners`: devices are numbered over seq and batch together, seq slowest. No device owns more than 10 panels, and some device owns exactly 10.
All inputs are finite; a program needn't handle non-finite values.
Results may differ from the reference program's by a relative error of at most 0.012.
Values may be sent and summed in bfloat16 or wider, within the bound.
No kernel may reach another device: no remote copies, remote signals or barrier semaphores. Data moves between devices by JAX's collectives and lax.ppermute only.
A program may use at most 192 MiB of HBM per device.

```python
import math
import jax
import jax.numpy as jnp
from jax import lax

D = 768
HEADS = 12
HEAD_DIM = 64
FF = 3072
BLOCK = 512
SEQ_DEV = 2
MIN_LEN = 64
PR = 32
SEQ_LEN = 1024
SEQS = 32
TOKENS = 32768
NP = 288
CAP = 10
SLOTS = 320
NS = 12


def slot_owners(key):
    slot_order = jax.random.permutation(jax.random.fold_in(key, 3), SLOTS).astype(jnp.int32)
    chosen_device = jax.random.randint(jax.random.fold_in(key, 5), (), 0, SLOTS // CAP)
    holder = slot_order // CAP
    priority = jnp.where(holder == chosen_device, -1, jnp.arange(SLOTS, dtype=jnp.int32))
    ranked = slot_order[jnp.argsort(priority, stable=True)]
    return (ranked[:NP] // CAP).astype(jnp.int32)


def panel_rows(key):
    owners = slot_owners(key)
    panel_index = jnp.arange(NP, dtype=jnp.int32)
    same_owner = (owners[:, None] == owners[None, :]) & (panel_index[None, :] < panel_index[:, None])
    rank_within = jnp.sum(same_owner.astype(jnp.int32), axis=1).astype(jnp.int32)
    slot_of = owners * CAP + rank_within
    return jnp.full((SLOTS,), 4 * D, jnp.int32).at[slot_of].set(panel_index * PR)


def slot_scales(key):
    first_row = panel_rows(key)
    weight_scale = jnp.where(first_row < 3 * D, D ** (-0.5), jnp.where(first_row < 4 * D, 0.25, jnp.where(first_row < 4 * D + FF, D ** (-0.5), FF ** (-0.5))))
    grad_factor = jnp.where(first_row < 3 * D, 0.5, jnp.where(first_row < 4 * D, 0.1, jnp.where(first_row < 4 * D + FF, 0.3, 0.6)))
    grad_scale = math.sqrt(TOKENS) * grad_factor
    return (weight_scale.astype(jnp.float32), grad_scale.astype(jnp.float32))


def signed_noise(key, dims):
    noise = jnp.clip(jax.random.normal(key, dims, jnp.float32), -4.0, 4.0)
    return noise


def draw_owners(key, part):
    return slot_owners(key)


def draw_lengths(key, part):
    group_total = SEQS // SEQ_DEV
    bucket_span = (SEQ_LEN - MIN_LEN) // 4
    bucket_level = jax.random.randint(jax.random.fold_in(key, 21), (group_total,), 0, 4)
    bucket_level = jnp.repeat(bucket_level, SEQ_DEV, total_repeat_length=SEQS)
    offset = jax.random.randint(jax.random.fold_in(key, 22), (SEQS,), 0, bucket_span + 1)
    drawn_lengths = MIN_LEN + bucket_level * bucket_span + offset
    seq_order = jax.random.permutation(jax.random.fold_in(key, 23), SEQS)
    drawn_lengths = drawn_lengths.at[seq_order[0]].set(SEQ_LEN).at[seq_order[1]].set(MIN_LEN)
    return drawn_lengths.astype(jnp.int32)


def draw_weight_slots(key, part):
    weight_scale, grad_scale = slot_scales(key)
    return weight_scale[:, None, None] * signed_noise(jax.random.fold_in(key, 11), (SLOTS, PR, D))


def draw_first_slots(key, part):
    weight_scale, grad_scale = slot_scales(key)
    return 0.111 * grad_scale[:, None, None] * signed_noise(jax.random.fold_in(key, 12), (SLOTS, PR, D))


def draw_second_slots(key, part):
    weight_scale, grad_scale = slot_scales(key)
    factor = jnp.exp(jax.random.uniform(jax.random.fold_in(key, 13), (SLOTS, PR, D), jnp.float32, math.log(0.5), math.log(8.0)))
    return 0.001 * factor * (grad_scale * grad_scale)[:, None, None]


def draw_small_params(key, part):
    noise = signed_noise(jax.random.fold_in(key, 14), (NS, D))
    row_number = jnp.arange(NS, dtype=jnp.int32)[:, None]
    is_gain = (row_number == 0) | (row_number == 2)
    return jnp.where(is_gain, 1.0 + 0.1 * noise, 0.1 * noise).astype(jnp.float32)


def block_levels(own_key, shape, split, smallest, high):
    def one(dim, blocks):
        steps = jax.random.uniform(jax.random.fold_in(jax.random.fold_in(own_key, 6), dim), (blocks,), jnp.float32, smallest / len(split), high / len(split))
        return jnp.repeat(jnp.exp(steps), shape[dim] // blocks).reshape((-1,) + (1,) * (len(shape) - dim - 1))

    factor_of = one(*split[0])
    for cut in split[1:]:
        factor_of = factor_of * one(*cut)
    return factor_of


def centred(stream_key, shape, scale, bound, cuts=(), kind=jnp.bfloat16):
    values = scale * jax.random.normal(stream_key, shape, jnp.float32)
    if cuts:
        values = values * block_levels(stream_key, shape, cuts, -0.22, 0.18)
    return jnp.clip(values, -bound, bound).astype(kind)


def setup_inputs(seed: int = 0) -> dict:
    key_list = jax.random.split(jax.random.key(seed), 12)
    return {
        "tokens": centred(key_list[0], (SEQS, SEQ_LEN, D), 1.0, 6.0, ((0, 16), (1, 2))),
        "grad_out": centred(key_list[1], (SEQS, SEQ_LEN, D), 1.0, 6.0, ((0, 16), (1, 2))),
        "lengths": draw_lengths(jax.random.fold_in(key_list[11], 71), 0),
        "owners": draw_owners(jax.random.fold_in(key_list[11], 71), 0),
        "weight_slots": draw_weight_slots(jax.random.fold_in(key_list[11], 71), 0),
        "first_slots": draw_first_slots(jax.random.fold_in(key_list[11], 71), 0),
        "second_slots": draw_second_slots(jax.random.fold_in(key_list[11], 71), 0),
        "small_params": draw_small_params(jax.random.fold_in(key_list[11], 71), 0),
        "small_first": centred(key_list[8], (NS, D), (0.09 * TOKENS ** 0.5), 96.0, (), jnp.float32),
        "small_second": jnp.clip(jnp.exp(jax.random.uniform(key_list[9], (NS, D), jnp.float32, math.log(9.8304), math.log(163.84))), 9.8304, 163.84),
        "step_count": jax.random.randint(key_list[10], (1,), 2, 8).astype(jnp.int32),
    }


@jax.custom_vjp
def low(v):
    return lax.optimization_barrier(v.astype(jnp.bfloat16)).astype(jnp.float32)

@jax.custom_vjp
def low_back(v):
    return v

def low_keep(v):
    return (low(v), None)

def low_pass(kept, grad):
    return (grad,)

def back_keep(v):
    return (v, None)

def back_low(kept, grad):
    return (low(grad),)
low.defvjp(low_keep, low_pass)
low_back.defvjp(back_keep, back_low)
highest = lax.Precision.HIGHEST
norm_eps = 1e-06
masked_score = -30.0
beta_first = 0.9
beta_second = 0.999
adam_eps = 1e-08
learn_rate = 0.2
decay_rate = 0.01

def matmul(left, right):
    return jnp.dot(left, right, precision=highest)

def slot_table(owners, capacity):
    panel_index = jnp.arange(owners.shape[0], dtype=jnp.int32)
    same_owner = (owners[:, None] == owners[None, :]) & (panel_index[None, :] < panel_index[:, None])
    rank_within = lax.optimization_barrier(jnp.sum(same_owner.astype(jnp.int32), axis=1)).astype(jnp.int32)
    return (owners * capacity + rank_within).astype(jnp.int32)

def layer_norm(values, gain_row, shift_row):
    centre = values - lax.optimization_barrier(jnp.mean(values, axis=-1, keepdims=True))
    spread = lax.optimization_barrier(jnp.mean(centre * centre, axis=-1, keepdims=True))
    return centre * lax.rsqrt(spread + norm_eps) * gain_row + shift_row

def adam_update(weight, first_old, second_old, grad_now, step_count):
    step_float = step_count[0].astype(jnp.float32)
    first_new = beta_first * first_old + (1.0 - beta_first) * grad_now
    second_new = beta_second * second_old + (1.0 - beta_second) * grad_now * grad_now
    first_hat = first_new / (1.0 - jnp.power(beta_first, step_float))
    second_hat = second_new / (1.0 - jnp.power(beta_second, step_float))
    weight_new = weight - learn_rate * (first_hat / (jnp.sqrt(second_hat) + adam_eps) + decay_rate * weight)
    return (weight_new, first_new, second_new)

def attend_block(block_items):
    queries, keys_low, values, live_keys = block_items
    scale_factor = 1.0 / math.sqrt(HEAD_DIM)
    scores = jnp.einsum('qhd,khd->hqk', queries, keys_low, precision=highest) * scale_factor
    scores = low_back(scores)
    scores = jnp.where(live_keys[None, None, :], scores, masked_score)
    probs_low = low(jax.nn.softmax(scores, axis=-1))
    context = jnp.einsum('hqk,khd->qhd', probs_low, values, precision=highest)
    return context.reshape(queries.shape[0], D)

def layer(weight_stack, small_params, block_in, seq_lengths):
    weights_low = low(weight_stack)
    w_query = weights_low[0:D]
    w_key = weights_low[D:2 * D]
    w_value = weights_low[2 * D:3 * D]
    w_out = weights_low[3 * D:4 * D]
    w_hidden = weights_low[4 * D:4 * D + FF]
    w_down = weights_low[4 * D + FF:]
    bias_hidden = small_params[8:].reshape(-1)
    group_size = block_in.shape[0]
    block_count = SEQ_LEN // BLOCK
    flat_tokens = block_in.reshape(-1, D)
    queries = low(low_back(matmul(flat_tokens, w_query) + small_params[4]))
    keys_low = low(low_back(matmul(flat_tokens, w_key)))
    values = low(low_back(matmul(flat_tokens, w_value) + small_params[5]))
    head_shape = (group_size * block_count, BLOCK, HEADS, HEAD_DIM)
    positions = jnp.arange(SEQ_LEN, dtype=jnp.int32).reshape(block_count, BLOCK)
    live_keys = (positions[None, :, :] < seq_lengths[:, None, None]).reshape(group_size * block_count, BLOCK)
    context = lax.map(jax.checkpoint(attend_block), (queries.reshape(head_shape), keys_low.reshape(head_shape), values.reshape(head_shape), live_keys))
    context = low(low_back(context.reshape(-1, D)))
    attn_out = low_back(matmul(context, w_out) + small_params[6])
    mixed_rows = layer_norm(flat_tokens + attn_out, small_params[0], small_params[1])
    mixed_rows = low(low_back(mixed_rows))
    hidden_pre = low_back(matmul(mixed_rows, w_hidden.T) + bias_hidden)
    hidden_low = low(jax.nn.gelu(hidden_pre, approximate=False))
    down_out = low_back(matmul(hidden_low, w_down) + small_params[7])
    result = layer_norm(mixed_rows + down_out, small_params[2], small_params[3])
    return result.reshape(block_in.shape)

def reference(tokens, grad_out, lengths, owners, weight_slots, first_slots, second_slots, small_params, small_first, small_second, step_count):
    slot_of = slot_table(owners, CAP)
    weight_stack = jnp.take(weight_slots, slot_of, axis=0).reshape(-1, D)
    group_size = 2 if SEQS % 2 == 0 else 1
    group_count = SEQS // group_size
    inputs = tokens.astype(jnp.float32).reshape(group_count, group_size, SEQ_LEN, D)
    cotangents = grad_out.astype(jnp.float32).reshape(group_count, group_size, SEQ_LEN, D)
    group_lengths = lengths.reshape(group_count, group_size)

    def one_group(carry_sums, block_items):
        stack_sum, small_sum = carry_sums
        block_in, block_cot, seq_lengths = block_items

        def forward(stack_now, small_now, input_now):
            return layer(stack_now, small_now, input_now, seq_lengths)
        result, pullback = jax.vjp(forward, weight_stack, small_params, block_in)
        d_stack, d_small, d_input = pullback(block_cot)
        return ((stack_sum + d_stack, small_sum + d_small), (result.astype(jnp.bfloat16), d_input))
    start_sums = (jnp.zeros(weight_stack.shape, jnp.float32), jnp.zeros(small_params.shape, jnp.float32))
    (grad_stack, small_grad), (outputs, input_grads) = lax.scan(one_group, start_sums, (inputs, cotangents, group_lengths))
    layer_out = outputs.reshape(SEQS, SEQ_LEN, D)
    grad_in = input_grads.reshape(SEQS, SEQ_LEN, D)
    panels = grad_stack.reshape(NP, PR, D)
    grad_slots = jnp.zeros((SLOTS, PR, D), jnp.float32).at[slot_of].set(panels)
    new_slots, new_first_slots, new_second_slots = adam_update(weight_slots, first_slots, second_slots, grad_slots, step_count)
    new_small, new_small_first, new_small_second = adam_update(small_params, small_first, small_second, small_grad, step_count)
    return (layer_out, grad_in, grad_slots, new_slots, new_first_slots, new_second_slots, small_grad, new_small, new_small_first, new_small_second)
```

```python
from functools import partial
import math

import jax
import jax.numpy as jnp
import numpy as np
from jax import lax
from jax.sharding import PartitionSpec as P

HEAD_DIM = 64


norm_eps = 1e-06
masked_score = -30.0
beta_first = 0.9
beta_second = 0.999
adam_eps = 1e-08
learn_rate = 0.2
decay_rate = 0.01


RING_ROUNDS = 5
LINKS = ("x", "y", "u", "d")
NEW_BLOCK = {
    (0, 0, "x"): (1, 0, 0), (0, 0, "y"): (0, 1, 0), (0, 0, "d"): (0, 0, 1),
    (0, 1, "x"): (1, 0, 1), (0, 1, "y"): (1, 1, 0), (0, 1, "d"): (0, 0, 2),
    (0, 2, "x"): (1, 0, 2), (0, 2, "y"): (0, 1, 2), (0, 2, "d"): (0, 0, 3),
    (0, 3, "x"): (1, 0, 3), (0, 3, "y"): (0, 1, 3), (0, 3, "d"): (1, 1, 2),
    (0, 4, "x"): (1, 1, 3), (0, 4, "y"): (1, 1, 1), (0, 4, "d"): (0, 1, 1),
    (1, 0, "x"): (1, 0, 1), (1, 0, "y"): (0, 1, 1), (1, 0, "u"): (0, 0, 0), (1, 0, "d"): (0, 0, 2),
    (1, 1, "x"): (1, 0, 2), (1, 1, "y"): (0, 1, 2), (1, 1, "u"): (1, 0, 0), (1, 1, "d"): (0, 0, 3),
    (1, 2, "x"): (1, 1, 2), (1, 2, "y"): (0, 1, 3), (1, 2, "u"): (0, 1, 0), (1, 2, "d"): (1, 0, 3),
    (1, 3, "x"): (1, 1, 0), (1, 3, "y"): (1, 1, 3), (1, 3, "d"): (1, 1, 1),
}
DUMMY = 16


def neighbour(chip, link):
    if link == "x":
        return chip ^ 1
    if link == "y":
        return chip ^ 2
    if link == "u":
        return chip - 4 if chip >= 4 else None
    return chip + 4 if chip < 12 else None


def received_block(chip, turn, link):
    layer = chip >> 2
    if layer < 2:
        block = NEW_BLOCK.get((layer, turn, link))
        if block is None:
            return None
        return block[2] * 4 + ((chip & 3) ^ (block[1] * 2 + block[0]))
    block = NEW_BLOCK.get((3 - layer, turn, {"u": "d", "d": "u"}.get(link, link)))
    if block is None:
        return None
    return (3 - block[2]) * 4 + ((chip & 3) ^ (block[1] * 2 + block[0]))


def build_schedule():
    rounds, columns = [], []
    for turn in range(RING_ROUNDS):
        moves = []
        for link in LINKS:
            pairs, takes, gives = [], [DUMMY] * 16, [DUMMY] * 16
            for chip in range(16):
                block = received_block(chip, turn, link)
                if block is None:
                    continue
                source = neighbour(chip, link)
                pairs.append((source, chip))
                takes[chip] = block
                gives[source] = block
            if pairs:
                moves.append((tuple(pairs), len(columns)))
                columns.append(takes)
                columns.append(gives)
        rounds.append(moves)
    return rounds, np.array(columns, np.int32).T


ROUNDS, TABLE = build_schedule()
SWAP = ((0, 1), (1, 0))


def schedule_row():
    return jnp.asarray(TABLE)[lax.axis_index("batch")]


def take_block(blocks, index):
    return lax.dynamic_index_in_dim(blocks, index, 0, keepdims=False)


def put_block(blocks, block, index):
    return lax.dynamic_update_index_in_dim(blocks, block, index, 0)


def gather_blocks(own):
    row = schedule_row()
    me = lax.axis_index("batch")
    both = jnp.zeros((2 * (DUMMY + 1),) + own.shape, own.dtype)
    both = put_block(both, own, me)
    both = put_block(both, lax.ppermute(own, "seq", SWAP), DUMMY + 1 + me)
    for turn, moves in enumerate(ROUNDS):
        arrived = []
        for pairs, column in moves:
            give = own if turn == 0 else take_block(both, row[column + 1])
            arrived.append((lax.ppermute(give, "batch", pairs), row[column]))
        for block, place in arrived:
            both = put_block(both, block, place)
            both = put_block(both, lax.ppermute(block, "seq", SWAP), DUMMY + 1 + place)
    return both


def reduce_blocks(blocks):
    row = schedule_row()
    me = lax.axis_index("batch")
    for turn in reversed(range(RING_ROUNDS)):
        arrived = []
        for pairs, column in ROUNDS[turn]:
            give = take_block(blocks, row[column])
            back = tuple((target, source) for source, target in pairs)
            arrived.append((lax.ppermute(give, "batch", back), row[column + 1]))
        if turn > 0:
            for block, place in arrived:
                blocks = put_block(blocks, take_block(blocks, place) + block, place)
    total = take_block(blocks, me).astype(jnp.float32)
    for block, place in arrived:
        total = total + block.astype(jnp.float32)
    return total


def sum_everywhere(values):
    size = lax.axis_size("batch")
    bit = 1
    while bit < size:
        values = values + lax.ppermute(values, "batch", [(i, i ^ bit) for i in range(size)])
        bit *= 2
    return values + lax.ppermute(values, "seq", SWAP)


def slot_table(owners, capacity):
    panel_index = jnp.arange(owners.shape[0], dtype=jnp.int32)
    same_owner = (owners[:, None] == owners[None, :]) & (
        panel_index[None, :] < panel_index[:, None]
    )
    rank_within = jnp.sum(same_owner.astype(jnp.int32), axis=1)
    return owners * capacity + rank_within


def layer_norm(values, gain_row, shift_row):
    centre = values - jnp.mean(values, axis=-1, keepdims=True)
    spread = jnp.mean(centre * centre, axis=-1, keepdims=True)
    return centre * lax.rsqrt(spread + norm_eps) * gain_row + shift_row


def adam_update(weight, first_old, second_old, grad_now, step_count):
    step_float = step_count[0].astype(jnp.float32)
    first_new = beta_first * first_old + (1.0 - beta_first) * grad_now
    second_new = beta_second * second_old + (1.0 - beta_second) * grad_now * grad_now
    first_hat = first_new / (1.0 - jnp.power(beta_first, step_float))
    second_hat = second_new / (1.0 - jnp.power(beta_second, step_float))
    weight_new = weight - learn_rate * (
        first_hat / (jnp.sqrt(second_hat) + adam_eps) + decay_rate * weight
    )
    return (weight_new, first_new, second_new)


def product(left, right):
    return jnp.dot(left, right, preferred_element_type=jnp.float32)


def contract_rows(left, right):
    return lax.dot_general(
        left, right, (((0,), (0,)), ((), ())), preferred_element_type=jnp.float32
    )


def contract_cols(left, right):
    return lax.dot_general(
        left, right, (((1,), (1,)), ((), ())), preferred_element_type=jnp.float32
    )


def column_sum(matrix):
    return jnp.sum(matrix, axis=0, dtype=jnp.float32)


def local(
    tokens,
    grad_out,
    lengths,
    owners,
    weight_slots,
    first_slots,
    second_slots,
    small_params,
    small_first,
    small_second,
    step_count,
):
    capacity = weight_slots.shape[0]
    seq_count, block_rows, features = tokens.shape
    head_count = features // HEAD_DIM
    scale_factor = 1.0 / math.sqrt(HEAD_DIM)
    hidden_width = (small_params.shape[0] - 8) * features
    slot_of = slot_table(owners, capacity)
    sending = weight_slots.astype(jnp.bfloat16)
    custom = lax.axis_size("batch") == 16 and lax.axis_size("seq") == 2
    if custom:
        gathered = gather_blocks(sending).reshape((-1,) + sending.shape[1:])
        rank = slot_of - owners * capacity
        other = (owners // 16) != lax.axis_index("seq")
        place = (jnp.where(other, DUMMY + 1, 0) + owners % 16) * capacity + rank
    else:
        gathered = lax.all_gather(sending, ("seq", "batch"), axis=0, tiled=True)
        place = slot_of
    weight_stack = jnp.take(gathered, place, axis=0).reshape(-1, features)
    w_query = weight_stack[0:features]
    w_key = weight_stack[features : 2 * features]
    w_value = weight_stack[2 * features : 3 * features]
    w_out = weight_stack[3 * features : 4 * features]
    w_hidden = weight_stack[4 * features : 4 * features + hidden_width]
    w_down = weight_stack[4 * features + hidden_width :]
    gain_one = small_params[0]
    shift_one = small_params[1]
    gain_two = small_params[2]
    shift_two = small_params[3]
    bias_hidden = small_params[8:].reshape(-1)
    flat_tokens = tokens.reshape(-1, features)
    tokens_wide = flat_tokens.astype(jnp.float32)
    queries = (product(flat_tokens, w_query) + small_params[4]).astype(jnp.bfloat16)
    keys_low = product(flat_tokens, w_key).astype(jnp.bfloat16)
    values = (product(flat_tokens, w_value) + small_params[5]).astype(jnp.bfloat16)
    positions = lax.axis_index("seq") * block_rows + jnp.arange(block_rows, dtype=jnp.int32)
    live_keys = positions[None, :] < lengths[:, None]

    def split_heads(matrix):
        return matrix.reshape(seq_count, block_rows, head_count, HEAD_DIM)

    def block_scores(query_heads, key_heads, live_row):
        scores = (
            jnp.einsum("qhd,khd->hqk", query_heads, key_heads, preferred_element_type=jnp.float32)
            * scale_factor
        )
        return jnp.where(live_row[None, None, :], scores, masked_score)

    def attend(block_items):
        query_heads, key_heads, value_heads, live_row = block_items
        scores = block_scores(query_heads, key_heads, live_row)
        row_top = jnp.max(scores, axis=-1, keepdims=True)
        exp_scores = jnp.exp(scores - row_top)
        exp_total = jnp.sum(exp_scores, axis=-1, keepdims=True)
        probs_low = (exp_scores / exp_total).astype(jnp.bfloat16)
        context = jnp.einsum(
            "hqk,khd->qhd", probs_low, value_heads, preferred_element_type=jnp.float32
        )
        return (
            context.reshape(block_rows, features).astype(jnp.bfloat16),
            (row_top + jnp.log(exp_total))[..., 0],
        )

    context, log_total = lax.map(
        attend, (split_heads(queries), split_heads(keys_low), split_heads(values), live_keys)
    )
    context_flat = context.reshape(-1, features)
    attn_out = product(context_flat, w_out) + small_params[6]
    mixed_rows, norm_one_pull = jax.vjp(layer_norm, tokens_wide + attn_out, gain_one, shift_one)
    mixed_low = mixed_rows.astype(jnp.bfloat16).reshape(tokens.shape)
    ffn_in, cot_in = mixed_low, grad_out
    ffn_rows = ffn_in.reshape(-1, features)
    cot_rows = cot_in.reshape(-1, features).astype(jnp.float32)
    hidden_pre = contract_cols(ffn_rows, w_hidden) + bias_hidden
    hidden_act, gelu_pull = jax.vjp(partial(jax.nn.gelu, approximate=False), hidden_pre)
    hidden_low = hidden_act.astype(jnp.bfloat16)
    residual = ffn_rows.astype(jnp.float32) + product(hidden_low, w_down) + small_params[7]
    layer_rows, norm_two_pull = jax.vjp(layer_norm, residual, gain_two, shift_two)
    d_residual, d_gain_two, d_shift_two = norm_two_pull(cot_rows)
    d_down = d_residual.astype(jnp.bfloat16)
    d_w_down = contract_rows(hidden_low, d_down)
    d_pre = gelu_pull(contract_cols(d_down, w_down))[0].astype(jnp.bfloat16)
    d_w_hidden = contract_rows(d_pre, ffn_rows)
    d_ffn_in = (d_residual + product(d_pre, w_hidden)).astype(jnp.bfloat16).reshape(ffn_in.shape)
    layer_low = layer_rows.astype(jnp.bfloat16).reshape(ffn_in.shape)
    layer_out, d_mixed = layer_low, d_ffn_in
    d_summed, d_gain_one, d_shift_one = norm_one_pull(
        d_mixed.reshape(-1, features).astype(jnp.float32)
    )
    d_attn = d_summed.astype(jnp.bfloat16)
    d_w_out = contract_rows(context_flat, d_attn)
    d_context = contract_cols(d_attn, w_out).astype(jnp.bfloat16)

    def attend_back(block_items):
        query_heads, key_heads, value_heads, live_row, total_row, d_context_row = block_items
        scores = block_scores(query_heads, key_heads, live_row)
        probs = jnp.exp(scores - total_row[..., None])
        d_heads = d_context_row.reshape(block_rows, head_count, HEAD_DIM)
        d_probs = jnp.einsum(
            "qhd,khd->hqk", d_heads, value_heads, preferred_element_type=jnp.float32
        )
        row_delta = jnp.sum(probs * d_probs, axis=-1, keepdims=True)
        d_scores = jnp.where(live_row[None, None, :], probs * (d_probs - row_delta), 0.0).astype(
            jnp.bfloat16
        )
        d_query = (
            jnp.einsum("hqk,khd->qhd", d_scores, key_heads, preferred_element_type=jnp.float32)
            * scale_factor
        )
        d_key = (
            jnp.einsum("hqk,qhd->khd", d_scores, query_heads, preferred_element_type=jnp.float32)
            * scale_factor
        )
        d_value = jnp.einsum(
            "hqk,qhd->khd", probs.astype(jnp.bfloat16), d_heads, preferred_element_type=jnp.float32
        )
        query_out = d_query.reshape(block_rows, features).astype(jnp.bfloat16)
        key_out = d_key.reshape(block_rows, features).astype(jnp.bfloat16)
        value_out = d_value.reshape(block_rows, features).astype(jnp.bfloat16)
        return (query_out, key_out, value_out)

    d_query, d_key, d_value = lax.map(
        attend_back,
        (
            split_heads(queries),
            split_heads(keys_low),
            split_heads(values),
            live_keys,
            log_total,
            d_context.reshape(tokens.shape),
        ),
    )
    d_query = d_query.reshape(-1, features)
    d_key = d_key.reshape(-1, features)
    d_value = d_value.reshape(-1, features)
    grad_in = (
        d_summed
        + contract_cols(d_query, w_query)
        + contract_cols(d_key, w_key)
        + contract_cols(d_value, w_value)
    )
    grad_stack = jnp.concatenate(
        [
            contract_rows(flat_tokens, d_query),
            contract_rows(flat_tokens, d_key),
            contract_rows(flat_tokens, d_value),
            d_w_out,
            d_w_hidden,
            d_w_down,
        ],
        axis=0,
    )
    panels = grad_stack.reshape(-1, weight_slots.shape[1], features)
    devices = lax.axis_size("seq") * lax.axis_size("batch")
    panel_at = (
        jnp.full((devices * capacity,), panels.shape[0], jnp.int32)
        .at[slot_of]
        .set(jnp.arange(panels.shape[0], dtype=jnp.int32))
    )
    padded = jnp.concatenate(
        [panels.astype(jnp.bfloat16), jnp.zeros((1,) + panels.shape[1:], jnp.bfloat16)], axis=0
    )
    slot_grads = jnp.take(padded, panel_at, axis=0)
    if custom:
        by_core = slot_grads.reshape((2, 16, capacity) + panels.shape[1:])
        core = lax.axis_index("seq")
        kept = take_block(by_core, core)
        blocks = kept + lax.ppermute(take_block(by_core, 1 - core), "seq", SWAP)
        blocks = jnp.concatenate([blocks, jnp.zeros_like(blocks[:1])], axis=0)
        grad_slots = reduce_blocks(blocks)
    else:
        grad_slots = lax.psum_scatter(
            slot_grads, ("seq", "batch"), scatter_dimension=0, tiled=True
        ).astype(jnp.float32)
    small_rows = jnp.stack(
        [
            d_gain_one,
            d_shift_one,
            d_gain_two,
            d_shift_two,
            column_sum(d_query),
            column_sum(d_value),
            column_sum(d_attn),
            column_sum(d_down),
        ]
    )
    small_local = jnp.concatenate([small_rows, column_sum(d_pre).reshape(-1, features)], axis=0)
    if custom:
        small_grad = sum_everywhere(small_local)
    else:
        small_grad = lax.psum(small_local, ("seq", "batch"))
    new_slots, new_first_slots, new_second_slots = adam_update(
        weight_slots, first_slots, second_slots, grad_slots, step_count
    )
    new_small, new_small_first, new_small_second = adam_update(
        small_params, small_first, small_second, small_grad, step_count
    )
    return (
        layer_out,
        grad_in.reshape(tokens.shape),
        grad_slots,
        new_slots,
        new_first_slots,
        new_second_slots,
        small_grad,
        new_small,
        new_small_first,
        new_small_second,
    )


def solution(mesh):
    in_specs = (
        P("batch", "seq", None),
        P("batch", "seq", None),
        P("batch"),
        P(),
        P(("seq", "batch"), None, None),
        P(("seq", "batch"), None, None),
        P(("seq", "batch"), None, None),
        P(),
        P(),
        P(),
        P(),
    )
    out_specs = (
        P("batch", "seq", None),
        P("batch", "seq", None),
        P(("seq", "batch"), None, None),
        P(("seq", "batch"), None, None),
        P(("seq", "batch"), None, None),
        P(("seq", "batch"), None, None),
        P(),
        P(),
        P(),
        P(),
    )
    return jax.shard_map(local, mesh=mesh, in_specs=in_specs, out_specs=out_specs, check_vma=False)
```

```python
from functools import partial
import math

import jax
import jax.numpy as jnp
import numpy as np
from jax import lax
from jax.experimental import pallas as pl
from jax.experimental.pallas import tpu as pltpu
from jax.sharding import PartitionSpec as P

beta_first = 0.9
beta_second = 0.999
adam_eps = 1e-08
learn_rate = 0.2
decay_rate = 0.01
SWAP = ((0, 1), (1, 0))

HEAD_DIM = 64
PANEL = 32
norm_eps = 1e-06
masked_score = -30.0
LANES = 128
BF = jnp.bfloat16
F32 = jnp.float32


def mm(a, b):
    return lax.dot_general(a, b, (((1,), (0,)), ((), ())), preferred_element_type=F32)


def mm_nt(a, b):
    return lax.dot_general(a, b, (((1,), (1,)), ((), ())), preferred_element_type=F32)


def mm_tn(a, b):
    return lax.dot_general(a, b, (((0,), (0,)), ((), ())), preferred_element_type=F32)


def normalize(z):
    centre = z - jnp.mean(z, axis=-1, keepdims=True)
    rstd = lax.rsqrt(jnp.mean(centre * centre, axis=-1, keepdims=True) + norm_eps)
    return centre * rstd, rstd


def norm_back(zh, rstd, t):
    mean_t = jnp.mean(t, axis=-1, keepdims=True)
    mean_tz = jnp.mean(t * zh, axis=-1, keepdims=True)
    return (t - mean_t - zh * mean_tz) * rstd


def lane_half(shape, half):
    lane = lax.broadcasted_iota(jnp.int32, shape, len(shape) - 1)
    return (lane < HEAD_DIM) if half == 0 else (lane >= HEAD_DIM)


def rows_of(panels, start, count):
    return panels[start // PANEL:(start + count) // PANEL].reshape(count, panels.shape[-1])


def fetch_panels(slots, first, target, place, sem):
    def one(i, carry):
        pltpu.make_async_copy(slots.at[place[first + i]], target.at[i], sem).start()
        return carry
    lax.fori_loop(0, target.shape[0], one, 0)


def fetch_wait(slots, target, sem):
    pltpu.make_async_copy(slots.at[pl.ds(0, target.shape[0])], target, sem).wait()


def send_panels(stage, first, slots, place, sem):
    def one(i, carry):
        pltpu.make_async_copy(stage.at[i], slots.at[place[first + i]], sem).start()
        return carry
    lax.fori_loop(0, stage.shape[0], one, 0)


def send_wait(stage, slots, sem):
    pltpu.make_async_copy(stage, slots.at[pl.ds(0, stage.shape[0])], sem).wait()


def attn_fwd_kernel(limits, place, x_ref, slots_ref, small_ref, q_ref, k_ref, v_ref, c_ref, p_ref,
                    mixed_ref, zh_ref, rstd_ref, w_ref, w_sem):
    step = pl.program_id(0)
    pairs = x_ref.shape[-1] // LANES
    seq, pair = step // pairs, step % pairs
    d = x_ref.shape[-1]
    block = x_ref.shape[1]

    @pl.when(step == 0)
    def _():
        fetch_panels(slots_ref, 0, w_ref, place, w_sem)
        fetch_wait(slots_ref, w_ref, w_sem)

    @pl.when(pair == 0)
    def _():
        x = x_ref[0]
        q = mm(x, rows_of(w_ref, 0, d)) + small_ref[4:5, :]
        q_ref[0] = (q.astype(BF).astype(F32) * 0.125).astype(BF)
        k_ref[0] = mm(x, rows_of(w_ref, d, d)).astype(BF)
        v_ref[0] = (mm(x, rows_of(w_ref, 2 * d, d)) + small_ref[5:6, :]).astype(BF)

    lanes = pl.ds(pl.multiple_of(pair * LANES, LANES), LANES)
    qp, kp, vp = q_ref[0, :, lanes], k_ref[0, :, lanes], v_ref[0, :, lanes]
    vt = vp.T
    limit = limits[seq]
    key = lax.broadcasted_iota(jnp.int32, (block, block), 0)
    parts = []
    for half in range(2):
        km = jnp.where(lane_half(kp.shape, half), kp, jnp.zeros_like(kp))
        s = mm_nt(km, qp)
        s = jnp.where(key < limit, s, masked_score)
        top = jnp.max(s, axis=0, keepdims=True)
        e = jnp.exp(s - top)
        total = jnp.sum(e, axis=0, keepdims=True)
        p = (e * (1.0 / total)).astype(BF)
        p_ref[half] = p
        parts.append(mm(vt[half * HEAD_DIM:(half + 1) * HEAD_DIM], p))
    ctx_t = jnp.concatenate(parts, axis=0)
    c_ref[0, :, lanes] = ctx_t.T.astype(BF)

    @pl.when(pair == pairs - 1)
    def _():
        u = x_ref[0].astype(F32) + mm(c_ref[0], rows_of(w_ref, 3 * d, d)) + small_ref[6:7, :]
        zh, rstd = normalize(u)
        zh_ref[0] = zh
        rstd_ref[0] = rstd
        mixed_ref[0] = (zh * small_ref[0:1, :] + small_ref[1:2, :]).astype(BF)


def attn_fwd(x, gathered, small, limits, place):
    seqs, block, d = x.shape
    pairs = d // LANES
    by_seq = lambda shape: pl.BlockSpec((1,) + shape, lambda i, lim, pr: (i // pairs, 0, 0))
    whole = lambda a: pl.BlockSpec(a, lambda i, lim, pr: (0, 0), pipeline_mode=pl.Buffered(1))
    act = jax.ShapeDtypeStruct((seqs, block, d), BF)
    return pl.pallas_call(
        attn_fwd_kernel,
        grid_spec=pltpu.PrefetchScalarGridSpec(
            num_scalar_prefetch=2,
            grid=(seqs * pairs,),
            in_specs=[by_seq((block, d)), pl.BlockSpec(memory_space=pl.ANY), whole(small.shape)],
            out_specs=[by_seq((block, d))] * 4
            + [pl.BlockSpec((2, block, block), lambda i, lim, pr: (i, 0, 0))]
            + [by_seq((block, d)), by_seq((block, d)), by_seq((block, 1))],
            scratch_shapes=[pltpu.VMEM((4 * d // PANEL, PANEL, d), BF), pltpu.SemaphoreType.DMA],
        ),
        out_shape=[act, act, act, act,
                   jax.ShapeDtypeStruct((seqs * 2 * pairs, block, block), BF),
                   act,
                   jax.ShapeDtypeStruct((seqs, block, d), F32),
                   jax.ShapeDtypeStruct((seqs, block, 1), F32)],
        compiler_params=pltpu.CompilerParams(vmem_limit_bytes=56 << 20, dimension_semantics=("arbitrary",)),
        name="attn_fwd",
    )(limits, place, x, gathered, small)


ROWS = 256
CHUNK = 512


def ffn_kernel(place, back, mixed_ref, go_ref, w_hbm, small_ref, bh_ref,
               out_ref, dmixed_ref, sums_ref, dbh_ref, slots_ref,
               w1, w2, hid, gp, acc, df, dyb, stage, w_sem, s_sem):
    d = mixed_ref.shape[-1]
    tokens = mixed_ref.shape[0]
    ff = bh_ref.shape[1]
    chunks = ff // CHUNK
    tiles = tokens // ROWS
    panels = CHUNK // PANEL
    first1 = 4 * d // PANEL
    first2 = first1 + ff // PANEL

    def start(c, carry):
        fetch_panels(w_hbm, first1 + c * panels, w1.at[c], place, w_sem.at[0, c])
        fetch_panels(w_hbm, first2 + c * panels, w2.at[c], place, w_sem.at[1, c])
        return carry

    lax.fori_loop(0, chunks, start, 0)

    def up(c, carry):
        fetch_wait(w_hbm, w1.at[c], w_sem.at[0, c])
        fetch_wait(w_hbm, w2.at[c], w_sem.at[1, c])
        cols = pl.ds(pl.multiple_of(c * CHUNK, CHUNK), CHUNK)
        w1c, w2c = w1[c].reshape(CHUNK, d), w2[c].reshape(CHUNK, d)
        bias = bh_ref[0:1, cols]
        for r in range(tiles):
            rows = pl.ds(r * ROWS, ROWS)
            f = mm_nt(mixed_ref[rows, :], w1c) + bias
            half_erf = 0.5 * lax.erf(f * (1.0 / math.sqrt(2.0))) + 0.5
            h = (f * half_erf).astype(BF)
            hid[rows, cols] = h
            gp[rows, cols] = (half_erf + f * (jnp.exp(-0.5 * f * f) * (1.0 / math.sqrt(2.0 * math.pi)))).astype(BF)
            part = mm(h, w2c)
            acc[rows, :] = jnp.where(c == 0, part, acc[rows, :] + part)
        return carry

    lax.fori_loop(0, chunks, up, 0)

    sums_ref[...] = jnp.zeros_like(sums_ref)

    def middle(r, carry):
        rows = pl.ds(pl.multiple_of(r * ROWS, ROWS), ROWS)
        rr = mixed_ref[rows, :].astype(F32) + acc[rows, :] + small_ref[7:8, :]
        zh, rstd = normalize(rr)
        out_ref[rows, :] = (zh * small_ref[2:3, :] + small_ref[3:4, :]).astype(BF)
        e = go_ref[rows, :].astype(F32)
        dr = norm_back(zh, rstd, e * small_ref[2:3, :])
        dy = dr.astype(BF)
        dyb[rows, :] = dy
        acc[rows, :] = dr
        sums_ref[0:1, :] += jnp.sum(e * zh, axis=0, keepdims=True)
        sums_ref[1:2, :] += jnp.sum(e, axis=0, keepdims=True)
        sums_ref[2:3, :] += jnp.sum(dy.astype(F32), axis=0, keepdims=True)
        return carry

    lax.fori_loop(0, tiles, middle, 0)

    def down(c, carry):
        cols = pl.ds(pl.multiple_of(c * CHUNK, CHUNK), CHUNK)
        w1c, w2c = w1[c].reshape(CHUNK, d), w2[c].reshape(CHUNK, d)
        dbh = jnp.zeros((1, CHUNK), F32)
        for r in range(tiles):
            rows = pl.ds(r * ROWS, ROWS)
            dfr = (mm_nt(dyb[rows, :], w2c) * gp[rows, cols].astype(F32)).astype(BF)
            df[rows, :] = dfr
            dbh += jnp.sum(dfr.astype(F32), axis=0, keepdims=True)
            acc[rows, :] += mm(dfr, w1c)
        dbh_ref[0:1, cols] = dbh

        @pl.when(c > 0)
        def _():
            send_wait(stage.at[0], slots_ref, s_sem.at[0])
            send_wait(stage.at[1], slots_ref, s_sem.at[1])

        stage[0] = mm_tn(df[...], mixed_ref[...]).astype(BF).reshape(panels, PANEL, d)
        send_panels(stage.at[0], first1 + c * panels, slots_ref, back, s_sem.at[0])
        stage[1] = mm_tn(hid[:, cols], dyb[...]).astype(BF).reshape(panels, PANEL, d)
        send_panels(stage.at[1], first2 + c * panels, slots_ref, back, s_sem.at[1])
        return carry

    lax.fori_loop(0, chunks, down, 0)
    dmixed_ref[...] = acc[...].astype(BF)
    send_wait(stage.at[0], slots_ref, s_sem.at[0])
    send_wait(stage.at[1], slots_ref, s_sem.at[1])


def ffn(mixed, go, gathered, small, bh, place, back, slots):
    tokens, d = mixed.shape
    ff = bh.shape[1]
    full = lambda shape: pl.BlockSpec(shape, lambda i, pr, bk: (0,) * len(shape))
    return pl.pallas_call(
        ffn_kernel,
        grid_spec=pltpu.PrefetchScalarGridSpec(
            num_scalar_prefetch=2,
            grid=(1,),
            in_specs=[full((tokens, d)), full((tokens, d)), pl.BlockSpec(memory_space=pl.ANY),
                      full(small.shape), full(bh.shape)],
            out_specs=[full((tokens, d)), full((tokens, d)), full((8, d)), full((1, ff)),
                       pl.BlockSpec(memory_space=pl.ANY)],
            scratch_shapes=[
                pltpu.VMEM((ff // CHUNK, CHUNK // PANEL, PANEL, d), BF),
                pltpu.VMEM((ff // CHUNK, CHUNK // PANEL, PANEL, d), BF),
                pltpu.VMEM((tokens, ff), BF), pltpu.VMEM((tokens, ff), BF),
                pltpu.VMEM((tokens, d), F32), pltpu.VMEM((tokens, CHUNK), BF),
                pltpu.VMEM((tokens, d), BF), pltpu.VMEM((2, CHUNK // PANEL, PANEL, d), BF),
                pltpu.SemaphoreType.DMA((2, ff // CHUNK)), pltpu.SemaphoreType.DMA((2,)),
            ],
        ),
        out_shape=[jax.ShapeDtypeStruct((tokens, d), BF), jax.ShapeDtypeStruct((tokens, d), BF),
                   jax.ShapeDtypeStruct((8, d), F32), jax.ShapeDtypeStruct((1, ff), F32),
                   jax.ShapeDtypeStruct((slots, PANEL, d), BF)],
        compiler_params=pltpu.CompilerParams(vmem_limit_bytes=60 << 20, dimension_semantics=("arbitrary",)),
        name="ffn",
    )(place, back, mixed, go, gathered, small, bh)


def attn_bwd_kernel(limits, place, back, dmixed_ref, zh_ref, rstd_ref, x_ref, q_ref, k_ref, v_ref,
                    c_ref, p_ref, w_hbm, small_ref, slots_in,
                    gin_ref, sums_ref, slots_ref,
                    dctx, dq, dk, dv, dw, stage, w_ref, s_sem, w_sem):
    step = pl.program_id(0)
    pairs = x_ref.shape[-1] // LANES
    seq, pair = step // pairs, step % pairs
    d = x_ref.shape[-1]
    block = x_ref.shape[1]
    tiles = block // ROWS

    @pl.when(step == 0)
    def _():
        fetch_panels(w_hbm, 0, w_ref, place, w_sem)
        dw[...] = jnp.zeros_like(dw)
        sums_ref[...] = jnp.zeros_like(sums_ref)
        fetch_wait(w_hbm, w_ref, w_sem)

    @pl.when(pair == 0)
    def _():
        for r in range(tiles):
            rows = pl.ds(r * ROWS, ROWS)
            e = dmixed_ref[0, rows, :].astype(F32)
            zh = zh_ref[0, rows, :]
            du = norm_back(zh, rstd_ref[0, rows, :], e * small_ref[0:1, :])
            da = du.astype(BF)
            gin_ref[0, rows, :] = du
            sums_ref[0:1, :] += jnp.sum(e * zh, axis=0, keepdims=True)
            sums_ref[1:2, :] += jnp.sum(e, axis=0, keepdims=True)
            sums_ref[4:5, :] += jnp.sum(da.astype(F32), axis=0, keepdims=True)
            dctx[rows, :] = mm_nt(da, rows_of(w_ref, 3 * d, d)).astype(BF)
            dw[pl.ds(3 * d, d), :] += mm_tn(c_ref[0, rows, :], da)

    lanes = pl.ds(pl.multiple_of(pair * LANES, LANES), LANES)
    qp, kp, vp, dcp = q_ref[0, :, lanes], k_ref[0, :, lanes], v_ref[0, :, lanes], dctx[:, lanes]
    kt = kp.T
    limit = limits[seq]
    key = lax.broadcasted_iota(jnp.int32, (block, block), 0)
    prod_t = (dcp.astype(F32) * c_ref[0, :, lanes].astype(F32)).T
    dqt, dks, dvs = [], [], []
    for half in range(2):
        vm = jnp.where(lane_half(vp.shape, half), vp, jnp.zeros_like(vp))
        dp = mm_nt(vm, dcp)
        delta = jnp.sum(prod_t[half * HEAD_DIM:(half + 1) * HEAD_DIM], axis=0, keepdims=True)
        p = p_ref[half]
        ds = jnp.where(key < limit, p.astype(F32) * (dp - delta), 0.0).astype(BF)
        dqt.append(mm(kt[half * HEAD_DIM:(half + 1) * HEAD_DIM], ds))
        dks.append(mm(ds, qp))
        dvs.append(mm(p, dcp))
    low = lane_half(qp.shape, 0)
    dq[:, lanes] = (jnp.concatenate(dqt, axis=0) * 0.125).T.astype(BF)
    dk[:, lanes] = jnp.where(low, dks[0], dks[1]).astype(BF)
    dv[:, lanes] = jnp.where(low, dvs[0], dvs[1]).astype(BF)

    @pl.when(pair == pairs - 1)
    def _():
        x = x_ref[0]
        gin_ref[0] += (mm_nt(dq[...], rows_of(w_ref, 0, d)) + mm_nt(dk[...], rows_of(w_ref, d, d))
                       + mm_nt(dv[...], rows_of(w_ref, 2 * d, d)))
        dw[pl.ds(0, d), :] += mm_tn(x, dq[...])
        dw[pl.ds(d, d), :] += mm_tn(x, dk[...])
        dw[pl.ds(2 * d, d), :] += mm_tn(x, dv[...])
        sums_ref[2:3, :] += jnp.sum(dq[...].astype(F32), axis=0, keepdims=True)
        sums_ref[3:4, :] += jnp.sum(dv[...].astype(F32), axis=0, keepdims=True)

    @pl.when(step == pl.num_programs(0) - 1)
    def _():
        stage[...] = dw[...].astype(BF).reshape(stage.shape)
        send_panels(stage, 0, slots_ref, back, s_sem)
        send_wait(stage, slots_ref, s_sem)


def attn_bwd(dmixed, zh, rstd, x, q, k, v, c, p, gathered, small, limits, place, back, slots):
    seqs, block, d = x.shape
    pairs = d // LANES
    by_seq = lambda shape: pl.BlockSpec((1,) + shape, lambda i, lim, pr, bk: (i // pairs, 0, 0))
    whole = lambda a: pl.BlockSpec(a, lambda i, lim, pr, bk: (0, 0), pipeline_mode=pl.Buffered(1))
    return pl.pallas_call(
        attn_bwd_kernel,
        grid_spec=pltpu.PrefetchScalarGridSpec(
            num_scalar_prefetch=3,
            grid=(seqs * pairs,),
            in_specs=[by_seq((block, d)), by_seq((block, d)), by_seq((block, 1))]
            + [by_seq((block, d))] * 5
            + [pl.BlockSpec((2, block, block), lambda i, lim, pr, bk: (i, 0, 0)),
               pl.BlockSpec(memory_space=pl.ANY), whole(small.shape), pl.BlockSpec(memory_space=pl.ANY)],
            out_specs=[by_seq((block, d)), pl.BlockSpec((8, d), lambda i, lim, pr, bk: (0, 0)),
                       pl.BlockSpec(memory_space=pl.ANY)],
            scratch_shapes=[pltpu.VMEM((block, d), BF)] * 4
            + [pltpu.VMEM((4 * d, d), F32), pltpu.VMEM((4 * d // PANEL, PANEL, d), BF),
               pltpu.VMEM((4 * d // PANEL, PANEL, d), BF), pltpu.SemaphoreType.DMA, pltpu.SemaphoreType.DMA],
        ),
        out_shape=[jax.ShapeDtypeStruct((seqs, block, d), F32), jax.ShapeDtypeStruct((8, d), F32),
                   jax.ShapeDtypeStruct(slots.shape, BF)],
        input_output_aliases={14: 2},
        compiler_params=pltpu.CompilerParams(vmem_limit_bytes=60 << 20, dimension_semantics=("arbitrary",)),
        name="attn_bwd",
    )(limits, place, back, dmixed, zh, rstd, x, q, k, v, c, p, gathered, small, slots)


def slot_table(owners, capacity):
    panel_index = jnp.arange(owners.shape[0], dtype=jnp.int32)
    same_owner = (owners[:, None] == owners[None, :]) & (
        panel_index[None, :] < panel_index[:, None]
    )
    rank_within = jnp.sum(same_owner.astype(jnp.int32), axis=1)
    return owners * capacity + rank_within


def adam_update(weight, first_old, second_old, grad_now, step_count):
    step_float = step_count[0].astype(jnp.float32)
    first_new = beta_first * first_old + (1.0 - beta_first) * grad_now
    second_new = beta_second * second_old + (1.0 - beta_second) * grad_now * grad_now
    first_hat = first_new / (1.0 - jnp.power(beta_first, step_float))
    second_hat = second_new / (1.0 - jnp.power(beta_second, step_float))
    weight_new = weight - learn_rate * (
        first_hat / (jnp.sqrt(second_hat) + adam_eps) + decay_rate * weight
    )
    return (weight_new, first_new, second_new)


def sum_everywhere(values):
    size = lax.axis_size("batch")
    bit = 1
    while bit < size:
        values = values + lax.ppermute(values, "batch", [(i, i ^ bit) for i in range(size)])
        bit *= 2
    return values + lax.ppermute(values, "seq", SWAP)


def local(
    tokens,
    grad_out,
    lengths,
    owners,
    weight_slots,
    first_slots,
    second_slots,
    small_params,
    small_first,
    small_second,
    step_count,
):
    capacity = weight_slots.shape[0]
    block_rows, features = tokens.shape[1:]
    slot_of = slot_table(owners, capacity)
    devices = lax.axis_size("seq") * lax.axis_size("batch")
    device = lax.axis_index("seq") * lax.axis_size("batch") + lax.axis_index("batch")
    limits = lengths - lax.axis_index("seq") * block_rows
    gathered = lax.all_gather(weight_slots.astype(BF), ("seq", "batch"), axis=0, tiled=True)
    q, k, v, ctx, probs, mixed, zh, rstd = attn_fwd(tokens, gathered, small_params, limits, slot_of)
    bias_hidden = small_params[8:].reshape(1, -1)
    layer_out, d_mixed, sums_ffn, d_bias, slots = ffn(
        mixed.reshape(-1, features), grad_out.reshape(-1, features), gathered, small_params,
        bias_hidden, slot_of, slot_of, devices * capacity)
    grad_in, sums_attn, slots = attn_bwd(
        d_mixed.reshape(tokens.shape), zh, rstd, tokens, q, k, v, ctx, probs, gathered,
        small_params, limits, slot_of, slot_of, slots)
    grad_slots = lax.psum_scatter(
        slots, ("seq", "batch"), scatter_dimension=0, tiled=True).astype(jnp.float32)
    held = jnp.sum((owners == device).astype(jnp.int32))
    used = jnp.arange(capacity, dtype=jnp.int32) < held
    grad_slots = jnp.where(used[:, None, None], grad_slots, 0.0)
    small_local = jnp.concatenate(
        [sums_attn[0:2], sums_ffn[0:2], sums_attn[2:5], sums_ffn[2:3],
         d_bias.reshape(-1, features)], axis=0)
    small_grad = sum_everywhere(small_local)
    new_slots, new_first_slots, new_second_slots = adam_update(
        weight_slots, first_slots, second_slots, grad_slots, step_count
    )
    new_small, new_small_first, new_small_second = adam_update(
        small_params, small_first, small_second, small_grad, step_count
    )
    return (
        layer_out.reshape(tokens.shape),
        grad_in,
        grad_slots,
        new_slots,
        new_first_slots,
        new_second_slots,
        small_grad,
        new_small,
        new_small_first,
        new_small_second,
    )


def solution(mesh):
    in_specs = (
        P("batch", "seq", None),
        P("batch", "seq", None),
        P("batch"),
        P(),
        P(("seq", "batch"), None, None),
        P(("seq", "batch"), None, None),
        P(("seq", "batch"), None, None),
        P(),
        P(),
        P(),
        P(),
    )
    out_specs = (
        P("batch", "seq", None),
        P("batch", "seq", None),
        P(("seq", "batch"), None, None),
        P(("seq", "batch"), None, None),
        P(("seq", "batch"), None, None),
        P(("seq", "batch"), None, None),
        P(),
        P(),
        P(),
        P(),
    )
    return jax.shard_map(local, mesh=mesh, in_specs=in_specs, out_specs=out_specs, check_vma=False)
```

```python
from functools import partial
import math

import jax
import jax.numpy as jnp
import numpy as np
from jax import lax
from jax.experimental import pallas as pl
from jax.experimental.pallas import tpu as pltpu
from jax.sharding import PartitionSpec as P

beta_first = 0.9
beta_second = 0.999
adam_eps = 1e-08
learn_rate = 0.2
decay_rate = 0.01
SWAP = ((0, 1), (1, 0))

HEAD_DIM = 64
PANEL = 32
norm_eps = 1e-06
masked_score = -30.0
LANES = 128
BF = jnp.bfloat16
F32 = jnp.float32
ANY = pl.BlockSpec(memory_space=pl.ANY)


def mm(a, b):
    return lax.dot_general(a, b, (((1,), (0,)), ((), ())), preferred_element_type=F32)


def mm_nt(a, b):
    return lax.dot_general(a, b, (((1,), (1,)), ((), ())), preferred_element_type=F32)


def mm_tn(a, b):
    return lax.dot_general(a, b, (((0,), (0,)), ((), ())), preferred_element_type=F32)


def normalize(z):
    centre = z - jnp.mean(z, axis=-1, keepdims=True)
    rstd = lax.rsqrt(jnp.mean(centre * centre, axis=-1, keepdims=True) + norm_eps)
    return centre * rstd, rstd


def norm_back(zh, rstd, t):
    mean_t = jnp.mean(t, axis=-1, keepdims=True)
    mean_tz = jnp.mean(t * zh, axis=-1, keepdims=True)
    return (t - mean_t - zh * mean_tz) * rstd


def lane_half(shape, half):
    lane = lax.broadcasted_iota(jnp.int32, shape, len(shape) - 1)
    return (lane < HEAD_DIM) if half == 0 else (lane >= HEAD_DIM)


def rows_of(panels, start, count):
    return panels[start // PANEL:(start + count) // PANEL].reshape(count, panels.shape[-1])


def fetch_panels(slots, first, target, place, sem):
    def one(i, carry):
        pltpu.make_async_copy(slots.at[place[first + i]], target.at[i], sem).start()
        return carry
    lax.fori_loop(0, target.shape[0], one, 0)


def fetch_wait(slots, target, sem):
    pltpu.make_async_copy(slots.at[pl.ds(0, target.shape[0])], target, sem).wait()


def send_panels(stage, first, mine, theirs, back, sem):
    half = mine.shape[0]

    def one(i, carry):
        slot = back[first + i]

        @pl.when(slot < half)
        def _():
            pltpu.make_async_copy(stage.at[i], mine.at[slot], sem).start()

        @pl.when(slot >= half)
        def _():
            pltpu.make_async_copy(stage.at[i], theirs.at[slot - half], sem).start()

        return carry

    lax.fori_loop(0, stage.shape[0], one, 0)


def send_wait(stage, mine, sem):
    pltpu.make_async_copy(stage, mine.at[pl.ds(0, stage.shape[0])], sem).wait()


def attn_fwd_kernel(limits, place, x_ref, slots_ref, small_ref, q_ref, k_ref, v_ref, c_ref, p_ref,
                    mixed_ref, zh_ref, rstd_ref, w_ref, w_sem):
    step = pl.program_id(0)
    groups = x_ref.shape[-1] // LANES // PAIRS_FWD
    seq, group = step // groups, step % groups
    d = x_ref.shape[-1]
    block = x_ref.shape[1]

    @pl.when(step == 0)
    def _():
        fetch_panels(slots_ref, 0, w_ref, place, w_sem)
        fetch_wait(slots_ref, w_ref, w_sem)

    @pl.when(group == 0)
    def _():
        x = x_ref[0]
        q = mm(x, rows_of(w_ref, 0, d)) + small_ref[4:5, :]
        q_ref[0] = (q.astype(BF).astype(F32) * 0.125).astype(BF)
        k_ref[0] = mm(x, rows_of(w_ref, d, d)).astype(BF)
        v_ref[0] = (mm(x, rows_of(w_ref, 2 * d, d)) + small_ref[5:6, :]).astype(BF)

    limit = limits[seq]
    key = lax.broadcasted_iota(jnp.int32, (block, block), 0)
    for n in range(PAIRS_FWD):
        lanes = pl.ds(pl.multiple_of((group * PAIRS_FWD + n) * LANES, LANES), LANES)
        qp, kp, vp = q_ref[0, :, lanes], k_ref[0, :, lanes], v_ref[0, :, lanes]
        vt = vp.T
        parts = []
        for half in range(2):
            km = jnp.where(lane_half(kp.shape, half), kp, jnp.zeros_like(kp))
            s = mm_nt(km, qp)
            s = jnp.where(key < limit, s, masked_score)
            top = jnp.max(s, axis=0, keepdims=True)
            e = jnp.exp(s - top)
            total = jnp.sum(e, axis=0, keepdims=True)
            p = (e * (1.0 / total)).astype(BF)
            p_ref[2 * n + half] = p
            parts.append(mm(vt[half * HEAD_DIM:(half + 1) * HEAD_DIM], p))
        ctx_t = jnp.concatenate(parts, axis=0)
        c_ref[0, :, lanes] = ctx_t.T.astype(BF)

    @pl.when(group == groups - 1)
    def _():
        u = x_ref[0].astype(F32) + mm(c_ref[0], rows_of(w_ref, 3 * d, d)) + small_ref[6:7, :]
        zh, rstd = normalize(u)
        zh_ref[0] = zh
        rstd_ref[0] = rstd
        mixed_ref[0] = (zh * small_ref[0:1, :] + small_ref[1:2, :]).astype(BF)


def attn_fwd(x, gathered, small, limits, place):
    seqs, block, d = x.shape
    pairs = d // LANES
    groups = pairs // PAIRS_FWD
    by_seq = lambda shape: pl.BlockSpec((1,) + shape, lambda i, lim, pr: (i // groups, 0, 0))
    whole = lambda a: pl.BlockSpec(a, lambda i, lim, pr: (0, 0), pipeline_mode=pl.Buffered(1))
    act = jax.ShapeDtypeStruct((seqs, block, d), BF)
    return pl.pallas_call(
        attn_fwd_kernel,
        grid_spec=pltpu.PrefetchScalarGridSpec(
            num_scalar_prefetch=2,
            grid=(seqs * groups,),
            in_specs=[by_seq((block, d)), ANY, whole(small.shape)],
            out_specs=[by_seq((block, d))] * 4
            + [pl.BlockSpec((2 * PAIRS_FWD, block, block), lambda i, lim, pr: (i, 0, 0))]
            + [by_seq((block, d)), by_seq((block, d)), by_seq((block, 1))],
            scratch_shapes=[pltpu.VMEM((4 * d // PANEL, PANEL, d), BF), pltpu.SemaphoreType.DMA],
        ),
        out_shape=[act, act, act, act,
                   jax.ShapeDtypeStruct((seqs * 2 * pairs, block, block), BF),
                   act,
                   jax.ShapeDtypeStruct((seqs, block, d), F32),
                   jax.ShapeDtypeStruct((seqs, block, 1), F32)],
        compiler_params=pltpu.CompilerParams(vmem_limit_bytes=56 << 20, dimension_semantics=("arbitrary",)),
        name="attn_fwd",
    )(limits, place, x, gathered, small)


ROWS = 512
PAIRS_FWD = 6
PAIRS_BWD = 3
CHUNK = 1024


def ffn_kernel(place, back, mixed_ref, go_ref, w_hbm, small_ref, bh_ref,
               out_ref, dmixed_ref, sums_ref, dbh_ref, mine, theirs,
               w1, w2, hid, gp, acc, df, dyb, stage, w_sem, s_sem):
    d = mixed_ref.shape[-1]
    tokens = mixed_ref.shape[0]
    ff = bh_ref.shape[1]
    chunks = ff // CHUNK
    tiles = tokens // ROWS
    panels = CHUNK // PANEL
    first1 = 4 * d // PANEL
    first2 = first1 + ff // PANEL

    def start(c, carry):
        fetch_panels(w_hbm, first1 + c * panels, w1.at[c], place, w_sem.at[0, c])
        fetch_panels(w_hbm, first2 + c * panels, w2.at[c], place, w_sem.at[1, c])
        return carry

    lax.fori_loop(0, chunks, start, 0)

    def up(c, carry):
        fetch_wait(w_hbm, w1.at[c], w_sem.at[0, c])
        fetch_wait(w_hbm, w2.at[c], w_sem.at[1, c])
        cols = pl.ds(pl.multiple_of(c * CHUNK, CHUNK), CHUNK)
        w1c, w2c = w1[c].reshape(CHUNK, d), w2[c].reshape(CHUNK, d)
        bias = bh_ref[0:1, cols]
        for r in range(tiles):
            rows = pl.ds(r * ROWS, ROWS)
            f = mm_nt(mixed_ref[rows, :], w1c) + bias
            half_erf = 0.5 * lax.erf(f * (1.0 / math.sqrt(2.0))) + 0.5
            h = (f * half_erf).astype(BF)
            hid[rows, cols] = h
            gp[rows, cols] = (half_erf + f * (jnp.exp(-0.5 * f * f) * (1.0 / math.sqrt(2.0 * math.pi)))).astype(BF)
            part = mm(h, w2c)
            acc[rows, :] = jnp.where(c == 0, part, acc[rows, :] + part)
        return carry

    lax.fori_loop(0, chunks, up, 0)

    sums_ref[...] = jnp.zeros_like(sums_ref)

    def middle(r, carry):
        rows = pl.ds(pl.multiple_of(r * ROWS, ROWS), ROWS)
        rr = mixed_ref[rows, :].astype(F32) + acc[rows, :] + small_ref[7:8, :]
        zh, rstd = normalize(rr)
        out_ref[rows, :] = (zh * small_ref[2:3, :] + small_ref[3:4, :]).astype(BF)
        e = go_ref[rows, :].astype(F32)
        dr = norm_back(zh, rstd, e * small_ref[2:3, :])
        dy = dr.astype(BF)
        dyb[rows, :] = dy
        acc[rows, :] = dr
        sums_ref[0:1, :] += jnp.sum(e * zh, axis=0, keepdims=True)
        sums_ref[1:2, :] += jnp.sum(e, axis=0, keepdims=True)
        sums_ref[2:3, :] += jnp.sum(dy.astype(F32), axis=0, keepdims=True)
        return carry

    lax.fori_loop(0, tiles, middle, 0)

    def down(c, carry):
        cols = pl.ds(pl.multiple_of(c * CHUNK, CHUNK), CHUNK)
        w1c, w2c = w1[c].reshape(CHUNK, d), w2[c].reshape(CHUNK, d)
        dbh = jnp.zeros((1, CHUNK), F32)
        for r in range(tiles):
            rows = pl.ds(r * ROWS, ROWS)
            dfr = (mm_nt(dyb[rows, :], w2c) * gp[rows, cols].astype(F32)).astype(BF)
            df[rows, :] = dfr
            dbh += jnp.sum(dfr.astype(F32), axis=0, keepdims=True)
            acc[rows, :] += mm(dfr, w1c)
        dbh_ref[0:1, cols] = dbh

        @pl.when(c > 0)
        def _():
            send_wait(stage.at[0], mine, s_sem.at[0])
            send_wait(stage.at[1], mine, s_sem.at[1])

        stage[0] = mm_tn(df[...], mixed_ref[...]).astype(BF).reshape(panels, PANEL, d)
        send_panels(stage.at[0], first1 + c * panels, mine, theirs, back, s_sem.at[0])
        stage[1] = mm_tn(hid[:, cols], dyb[...]).astype(BF).reshape(panels, PANEL, d)
        send_panels(stage.at[1], first2 + c * panels, mine, theirs, back, s_sem.at[1])
        return carry

    lax.fori_loop(0, chunks, down, 0)
    dmixed_ref[...] = acc[...].astype(BF)
    send_wait(stage.at[0], mine, s_sem.at[0])
    send_wait(stage.at[1], mine, s_sem.at[1])


def ffn(mixed, go, gathered, small, bh, place, back, half):
    tokens, d = mixed.shape
    ff = bh.shape[1]
    full = lambda shape: pl.BlockSpec(shape, lambda i, pr, bk: (0,) * len(shape))
    return pl.pallas_call(
        ffn_kernel,
        grid_spec=pltpu.PrefetchScalarGridSpec(
            num_scalar_prefetch=2,
            grid=(1,),
            in_specs=[full((tokens, d)), full((tokens, d)), ANY,
                      full(small.shape), full(bh.shape)],
            out_specs=[full((tokens, d)), full((tokens, d)), full((8, d)), full((1, ff)),
                       ANY, ANY],
            scratch_shapes=[
                pltpu.VMEM((ff // CHUNK, CHUNK // PANEL, PANEL, d), BF),
                pltpu.VMEM((ff // CHUNK, CHUNK // PANEL, PANEL, d), BF),
                pltpu.VMEM((tokens, ff), BF), pltpu.VMEM((tokens, ff), BF),
                pltpu.VMEM((tokens, d), F32), pltpu.VMEM((tokens, CHUNK), BF),
                pltpu.VMEM((tokens, d), BF), pltpu.VMEM((2, CHUNK // PANEL, PANEL, d), BF),
                pltpu.SemaphoreType.DMA((2, ff // CHUNK)), pltpu.SemaphoreType.DMA((2,)),
            ],
        ),
        out_shape=[jax.ShapeDtypeStruct((tokens, d), BF), jax.ShapeDtypeStruct((tokens, d), BF),
                   jax.ShapeDtypeStruct((8, d), F32), jax.ShapeDtypeStruct((1, ff), F32),
                   jax.ShapeDtypeStruct((half, PANEL, d), BF), jax.ShapeDtypeStruct((half, PANEL, d), BF)],
        compiler_params=pltpu.CompilerParams(vmem_limit_bytes=60 << 20, dimension_semantics=("arbitrary",)),
        name="ffn",
    )(place, back, mixed, go, gathered, small, bh)


def attn_bwd_kernel(limits, place, back, dmixed_ref, zh_ref, rstd_ref, x_ref, q_ref, k_ref, v_ref,
                    c_ref, p_ref, w_hbm, small_ref, mine_in, theirs_in,
                    gin_ref, sums_ref, mine, theirs,
                    dctx, dq, dk, dv, dw, stage, w_ref, s_sem, w_sem):
    step = pl.program_id(0)
    groups = x_ref.shape[-1] // LANES // PAIRS_BWD
    seq, group = step // groups, step % groups
    d = x_ref.shape[-1]
    block = x_ref.shape[1]
    tiles = block // ROWS

    @pl.when(step == 0)
    def _():
        fetch_panels(w_hbm, 0, w_ref, place, w_sem)
        dw[...] = jnp.zeros_like(dw)
        sums_ref[...] = jnp.zeros_like(sums_ref)
        fetch_wait(w_hbm, w_ref, w_sem)

    @pl.when(group == 0)
    def _():
        for r in range(tiles):
            rows = pl.ds(r * ROWS, ROWS)
            e = dmixed_ref[0, rows, :].astype(F32)
            zh = zh_ref[0, rows, :]
            du = norm_back(zh, rstd_ref[0, rows, :], e * small_ref[0:1, :])
            da = du.astype(BF)
            gin_ref[0, rows, :] = du
            sums_ref[0:1, :] += jnp.sum(e * zh, axis=0, keepdims=True)
            sums_ref[1:2, :] += jnp.sum(e, axis=0, keepdims=True)
            sums_ref[4:5, :] += jnp.sum(da.astype(F32), axis=0, keepdims=True)
            dctx[rows, :] = mm_nt(da, rows_of(w_ref, 3 * d, d)).astype(BF)
            dw[pl.ds(3 * d, d), :] += mm_tn(c_ref[0, rows, :], da)

    limit = limits[seq]
    key = lax.broadcasted_iota(jnp.int32, (block, block), 0)
    for n in range(PAIRS_BWD):
        lanes = pl.ds(pl.multiple_of((group * PAIRS_BWD + n) * LANES, LANES), LANES)
        qp, kp, vp, dcp = q_ref[0, :, lanes], k_ref[0, :, lanes], v_ref[0, :, lanes], dctx[:, lanes]
        kt = kp.T
        prod_t = (dcp.astype(F32) * c_ref[0, :, lanes].astype(F32)).T
        dqt, dks, dvs = [], [], []
        for half in range(2):
            vm = jnp.where(lane_half(vp.shape, half), vp, jnp.zeros_like(vp))
            dp = mm_nt(vm, dcp)
            delta = jnp.sum(prod_t[half * HEAD_DIM:(half + 1) * HEAD_DIM], axis=0, keepdims=True)
            p = p_ref[2 * n + half]
            ds = jnp.where(key < limit, p.astype(F32) * (dp - delta), 0.0).astype(BF)
            dqt.append(mm(kt[half * HEAD_DIM:(half + 1) * HEAD_DIM], ds))
            dks.append(mm(ds, qp))
            dvs.append(mm(p, dcp))
        low = lane_half(qp.shape, 0)
        dq[:, lanes] = (jnp.concatenate(dqt, axis=0) * 0.125).T.astype(BF)
        dk[:, lanes] = jnp.where(low, dks[0], dks[1]).astype(BF)
        dv[:, lanes] = jnp.where(low, dvs[0], dvs[1]).astype(BF)

    @pl.when(group == groups - 1)
    def _():
        x = x_ref[0]
        gin_ref[0] += (mm_nt(dq[...], rows_of(w_ref, 0, d)) + mm_nt(dk[...], rows_of(w_ref, d, d))
                       + mm_nt(dv[...], rows_of(w_ref, 2 * d, d)))
        dw[pl.ds(0, d), :] += mm_tn(x, dq[...])
        dw[pl.ds(d, d), :] += mm_tn(x, dk[...])
        dw[pl.ds(2 * d, d), :] += mm_tn(x, dv[...])
        sums_ref[2:3, :] += jnp.sum(dq[...].astype(F32), axis=0, keepdims=True)
        sums_ref[3:4, :] += jnp.sum(dv[...].astype(F32), axis=0, keepdims=True)

    @pl.when(step == pl.num_programs(0) - 1)
    def _():
        stage[...] = dw[...].astype(BF).reshape(stage.shape)
        send_panels(stage, 0, mine, theirs, back, s_sem)
        send_wait(stage, mine, s_sem)


def attn_bwd(dmixed, zh, rstd, x, q, k, v, c, p, gathered, small, limits, place, back, mine, theirs):
    seqs, block, d = x.shape
    pairs = d // LANES
    groups = pairs // PAIRS_BWD
    by_seq = lambda shape: pl.BlockSpec((1,) + shape, lambda i, lim, pr, bk: (i // groups, 0, 0))
    whole = lambda a: pl.BlockSpec(a, lambda i, lim, pr, bk: (0, 0), pipeline_mode=pl.Buffered(1))
    return pl.pallas_call(
        attn_bwd_kernel,
        grid_spec=pltpu.PrefetchScalarGridSpec(
            num_scalar_prefetch=3,
            grid=(seqs * groups,),
            in_specs=[by_seq((block, d)), by_seq((block, d)), by_seq((block, 1))]
            + [by_seq((block, d))] * 5
            + [pl.BlockSpec((2 * PAIRS_BWD, block, block), lambda i, lim, pr, bk: (i, 0, 0)),
               ANY, whole(small.shape), ANY, ANY],
            out_specs=[by_seq((block, d)), pl.BlockSpec((8, d), lambda i, lim, pr, bk: (0, 0)),
                       ANY, ANY],
            scratch_shapes=[pltpu.VMEM((block, d), BF)] * 4
            + [pltpu.VMEM((4 * d, d), F32), pltpu.VMEM((4 * d // PANEL, PANEL, d), BF),
               pltpu.VMEM((4 * d // PANEL, PANEL, d), BF), pltpu.SemaphoreType.DMA, pltpu.SemaphoreType.DMA],
        ),
        out_shape=[jax.ShapeDtypeStruct((seqs, block, d), F32), jax.ShapeDtypeStruct((8, d), F32),
                   jax.ShapeDtypeStruct(mine.shape, BF), jax.ShapeDtypeStruct(mine.shape, BF)],
        input_output_aliases={14: 2, 15: 3},
        compiler_params=pltpu.CompilerParams(vmem_limit_bytes=60 << 20, dimension_semantics=("arbitrary",)),
        name="attn_bwd",
    )(limits, place, back, dmixed, zh, rstd, x, q, k, v, c, p, gathered, small, mine, theirs)


RING_ROUNDS = 5
LINKS = ("x", "y", "u", "d")
NEW_BLOCK = {
    (0, 0, "x"): (1, 0, 0), (0, 0, "y"): (0, 1, 0), (0, 0, "d"): (0, 0, 1),
    (0, 1, "x"): (1, 0, 1), (0, 1, "y"): (1, 1, 0), (0, 1, "d"): (0, 0, 2),
    (0, 2, "x"): (1, 0, 2), (0, 2, "y"): (0, 1, 2), (0, 2, "d"): (0, 0, 3),
    (0, 3, "x"): (1, 0, 3), (0, 3, "y"): (0, 1, 3), (0, 3, "d"): (1, 1, 2),
    (0, 4, "x"): (1, 1, 3), (0, 4, "y"): (1, 1, 1), (0, 4, "d"): (0, 1, 1),
    (1, 0, "x"): (1, 0, 1), (1, 0, "y"): (0, 1, 1), (1, 0, "u"): (0, 0, 0), (1, 0, "d"): (0, 0, 2),
    (1, 1, "x"): (1, 0, 2), (1, 1, "y"): (0, 1, 2), (1, 1, "u"): (1, 0, 0), (1, 1, "d"): (0, 0, 3),
    (1, 2, "x"): (1, 1, 2), (1, 2, "y"): (0, 1, 3), (1, 2, "u"): (0, 1, 0), (1, 2, "d"): (1, 0, 3),
    (1, 3, "x"): (1, 1, 0), (1, 3, "y"): (1, 1, 3), (1, 3, "d"): (1, 1, 1),
}
DUMMY = 16


def neighbour(chip, link):
    if link == "x":
        return chip ^ 1
    if link == "y":
        return chip ^ 2
    if link == "u":
        return chip - 4 if chip >= 4 else None
    return chip + 4 if chip < 12 else None


def received_block(chip, turn, link):
    layer = chip >> 2
    if layer < 2:
        block = NEW_BLOCK.get((layer, turn, link))
        if block is None:
            return None
        return block[2] * 4 + ((chip & 3) ^ (block[1] * 2 + block[0]))
    block = NEW_BLOCK.get((3 - layer, turn, {"u": "d", "d": "u"}.get(link, link)))
    if block is None:
        return None
    return (3 - block[2]) * 4 + ((chip & 3) ^ (block[1] * 2 + block[0]))


def build_schedule():
    moves, columns = [], []
    held = [{chip: -1} for chip in range(16)]
    for turn in range(RING_ROUNDS):
        fresh = []
        for link in LINKS:
            pairs, takes, gives, given = [], [DUMMY] * 16, [DUMMY] * 16, {}
            for chip in range(16):
                block = received_block(chip, turn, link)
                if block is None:
                    continue
                source = neighbour(chip, link)
                pairs.append((source, chip))
                takes[chip] = block
                gives[source] = block
                given[source] = held[source][block]
                fresh.append((chip, block, len(moves)))
            if not pairs:
                continue
            sources = sorted(set(given.values()))
            which = [sources.index(given.get(chip, sources[0])) for chip in range(16)]
            moves.append((turn, link, tuple(pairs), tuple(sources)))
            columns += [takes, which, gives]
        for chip, block, move in fresh:
            held[chip][block] = move
    return moves, np.array(columns, np.int32).T


MOVES, TABLE = build_schedule()


def feeders(move):
    takes = [received_block(chip, MOVES[move][0], MOVES[move][1]) for chip in range(16)]
    return feeding(takes, MOVES[move][0])


def feeding(blocks, turn):
    found = []
    for later, (after, link, pairs, _) in enumerate(MOVES):
        if after <= turn:
            continue
        chips = [
            source for source, target in pairs
            if blocks[source] is not None and received_block(target, after, link) == blocks[source]
        ]
        if chips:
            found.append((later, tuple(chips)))
    return found


def build_feeds():
    feeds, columns = [], []
    for move in range(len(MOVES) + 1):
        found = feeders(move) if move < len(MOVES) else feeding(list(range(16)), -1)
        feeds.append([(later, len(columns) + i) for i, (later, _) in enumerate(found)])
        columns += [[int(chip in chips) for chip in range(16)] for _, chips in found]
    return feeds, np.array(columns, np.int32).T


FEEDS, FEED_TABLE = build_feeds()


def add_kernel(block_column, flags, row, feed, mine, pair, *refs):
    out, acc = refs[-2], refs[-1]
    acc[...] = mine[0].astype(F32) + pair[0].astype(F32)
    for ref, column in zip(refs[:-2], flags):
        @pl.when(feed[column] == 1)
        def _():
            acc[...] += ref[...].astype(F32)
    out[...] = acc[...].astype(out.dtype)


def add_block(row, feed, block_column, mine, pair, arrays, flags, dtype):
    slots = mine.shape[1]
    shape = mine.shape[1:]
    pieces = 2 if slots % 2 == 0 else 1
    piece = (slots // pieces,) + shape[1:]
    by_block = pl.BlockSpec((1,) + piece, lambda i, rw, fd: (rw[block_column], i, 0, 0))
    plain = pl.BlockSpec(piece, lambda i, rw, fd: (i, 0, 0))
    return pl.pallas_call(
        partial(add_kernel, block_column, tuple(flags)),
        grid_spec=pltpu.PrefetchScalarGridSpec(
            num_scalar_prefetch=2, grid=(pieces,),
            in_specs=[by_block, by_block] + [plain] * len(arrays), out_specs=plain,
            scratch_shapes=[pltpu.VMEM(piece, F32)]),
        out_shape=jax.ShapeDtypeStruct(shape, dtype),
        cost_estimate=pl.CostEstimate(
            flops=0, bytes_accessed=2 * mine[0].size * (3 + len(arrays)), transcendentals=0),
        compiler_params=pltpu.CompilerParams(vmem_limit_bytes=12 << 20),
        name="add_block",
    )(row, feed, mine, pair, *arrays)


def partners():
    size = lax.axis_size("batch")
    steps, bit = [], 1
    while bit < size:
        steps.append(("batch", tuple((i, i ^ bit) for i in range(size))))
        bit *= 2
    return steps + [("seq", SWAP)]


def reduce_slots(mine, theirs, small):
    me = lax.axis_index("batch")
    takes = jnp.asarray(TABLE)[me][0::3]
    row = jnp.concatenate([jnp.where(takes == DUMMY, 0, takes), jnp.stack([me])])
    feed = jnp.asarray(FEED_TABLE)[me]
    pair = lax.ppermute(theirs, "seq", SWAP)
    mine = mine.reshape((16, -1) + mine.shape[1:])
    pair = pair.reshape(mine.shape)
    steps = partners()
    early = small
    for step in (steps.pop(-2), steps.pop(-2)):
        early = early + lax.ppermute(early, *step)
    small = early
    arrived, ready = {}, lax.optimization_barrier((row, early))[0]
    for turn in reversed(range(RING_ROUNDS)):
        gives = []
        for i in [i for i, move in enumerate(MOVES) if move[0] == turn]:
            give = add_block(ready, feed, i, mine, pair, [arrived[m] for m, _ in FEEDS[i]],
                             [column for _, column in FEEDS[i]], BF)
            gives.append(give)
            back = tuple((target, source) for source, target in MOVES[i][2])
            arrived[i] = lax.ppermute(give, "batch", back)
        ready, small, *_ = lax.optimization_barrier((row, small, *gives))
        if steps:
            small = small + lax.ppermute(small, *steps.pop(0))
    for step in steps:
        small = small + lax.ppermute(small, *step)
    last = FEEDS[len(MOVES)]
    total = add_block(row, feed, len(MOVES), mine, pair, [arrived[m] for m, _ in last],
                      [column for _, column in last], F32)
    return total, small


def slot_table(owners, capacity):
    panel_index = jnp.arange(owners.shape[0], dtype=jnp.int32)
    same_owner = (owners[:, None] == owners[None, :]) & (
        panel_index[None, :] < panel_index[:, None]
    )
    rank_within = jnp.sum(same_owner.astype(jnp.int32), axis=1)
    return owners * capacity + rank_within


def adam_update(weight, first_old, second_old, grad_now, step_count):
    step_float = step_count[0].astype(jnp.float32)
    first_new = beta_first * first_old + (1.0 - beta_first) * grad_now
    second_new = beta_second * second_old + (1.0 - beta_second) * grad_now * grad_now
    first_hat = first_new / (1.0 - jnp.power(beta_first, step_float))
    second_hat = second_new / (1.0 - jnp.power(beta_second, step_float))
    weight_new = weight - learn_rate * (
        first_hat / (jnp.sqrt(second_hat) + adam_eps) + decay_rate * weight
    )
    return (weight_new, first_new, second_new)


def local(
    tokens,
    grad_out,
    lengths,
    owners,
    weight_slots,
    first_slots,
    second_slots,
    small_params,
    small_first,
    small_second,
    step_count,
):
    capacity = weight_slots.shape[0]
    block_rows, features = tokens.shape[1:]
    slot_of = slot_table(owners, capacity)
    devices = lax.axis_size("seq") * lax.axis_size("batch")
    device = lax.axis_index("seq") * lax.axis_size("batch") + lax.axis_index("batch")
    limits = lengths - lax.axis_index("seq") * block_rows
    core = lax.axis_index("seq")
    batch = lax.axis_size("batch")
    half = batch * capacity
    owner_core = (owners >= batch).astype(jnp.int32)
    back = slot_of - owner_core * half + jnp.where(owner_core == core, 0, half)
    gathered = lax.all_gather(weight_slots.astype(BF), ("seq", "batch"), axis=0, tiled=True)
    q, k, v, ctx, probs, mixed, zh, rstd = attn_fwd(tokens, gathered, small_params, limits, slot_of)
    bias_hidden = small_params[8:].reshape(1, -1)
    layer_out, d_mixed, sums_ffn, d_bias, mine, theirs = ffn(
        mixed.reshape(-1, features), grad_out.reshape(-1, features), gathered, small_params,
        bias_hidden, slot_of, back, half)
    grad_in, sums_attn, mine, theirs = attn_bwd(
        d_mixed.reshape(tokens.shape), zh, rstd, tokens, q, k, v, ctx, probs, gathered,
        small_params, limits, slot_of, back, mine, theirs)
    small_local = jnp.concatenate(
        [sums_attn[0:2], sums_ffn[0:2], sums_attn[2:5], sums_ffn[2:3],
         d_bias.reshape(-1, features)], axis=0)
    if batch == 16 and lax.axis_size("seq") == 2:
        grad_slots, small_grad = reduce_slots(mine, theirs, small_local)
    else:
        both = jnp.where(core == 0, jnp.stack([mine, theirs]), jnp.stack([theirs, mine]))
        grad_slots = lax.psum_scatter(
            both.reshape((-1,) + mine.shape[1:]), ("seq", "batch"), scatter_dimension=0,
            tiled=True).astype(jnp.float32)
        small_grad = small_local
        for step in partners():
            small_grad = small_grad + lax.ppermute(small_grad, *step)
    held = jnp.sum((owners == device).astype(jnp.int32))
    used = jnp.arange(capacity, dtype=jnp.int32) < held
    grad_slots = jnp.where(used[:, None, None], grad_slots, 0.0)
    new_slots, new_first_slots, new_second_slots = adam_update(
        weight_slots, first_slots, second_slots, grad_slots, step_count
    )
    new_small, new_small_first, new_small_second = adam_update(
        small_params, small_first, small_second, small_grad, step_count
    )
    return (
        layer_out.reshape(tokens.shape),
        grad_in,
        grad_slots,
        new_slots,
        new_first_slots,
        new_second_slots,
        small_grad,
        new_small,
        new_small_first,
        new_small_second,
    )


def solution(mesh):
    in_specs = (
        P("batch", "seq", None),
        P("batch", "seq", None),
        P("batch"),
        P(),
        P(("seq", "batch"), None, None),
        P(("seq", "batch"), None, None),
        P(("seq", "batch"), None, None),
        P(),
        P(),
        P(),
        P(),
    )
    out_specs = (
        P("batch", "seq", None),
        P("batch", "seq", None),
        P(("seq", "batch"), None, None),
        P(("seq", "batch"), None, None),
        P(("seq", "batch"), None, None),
        P(("seq", "batch"), None, None),
        P(),
        P(),
        P(),
        P(),
    )
    return jax.shard_map(local, mesh=mesh, in_specs=in_specs, out_specs=out_specs, check_vma=False)
```

```python
from functools import partial
import math

import jax
import jax.numpy as jnp
import numpy as np
from jax import lax
from jax.experimental import pallas as pl
from jax.experimental.pallas import tpu as pltpu
from jax.sharding import PartitionSpec as P

beta_first = 0.9
beta_second = 0.999
adam_eps = 1e-08
learn_rate = 0.2
decay_rate = 0.01
SWAP = ((0, 1), (1, 0))

HEAD_DIM = 64
PANEL = 32
norm_eps = 1e-06
masked_score = -30.0
LANES = 128
BF = jnp.bfloat16
F32 = jnp.float32
ANY = pl.BlockSpec(memory_space=pl.ANY)


def mm(a, b):
    return lax.dot_general(a, b, (((1,), (0,)), ((), ())), preferred_element_type=F32)


def mm_nt(a, b):
    return lax.dot_general(a, b, (((1,), (1,)), ((), ())), preferred_element_type=F32)


def mm_tn(a, b):
    return lax.dot_general(a, b, (((0,), (0,)), ((), ())), preferred_element_type=F32)


def normalize(z):
    centre = z - jnp.mean(z, axis=-1, keepdims=True)
    rstd = lax.rsqrt(jnp.mean(centre * centre, axis=-1, keepdims=True) + norm_eps)
    return centre * rstd, rstd


def norm_back(zh, rstd, t):
    mean_t = jnp.mean(t, axis=-1, keepdims=True)
    mean_tz = jnp.mean(t * zh, axis=-1, keepdims=True)
    return (t - mean_t - zh * mean_tz) * rstd


def lane_half(shape, half):
    lane = lax.broadcasted_iota(jnp.int32, shape, len(shape) - 1)
    return (lane < HEAD_DIM) if half == 0 else (lane >= HEAD_DIM)


def rows_of(panels, start, count):
    return panels[start // PANEL:(start + count) // PANEL].reshape(count, panels.shape[-1])


def fetch_panels(slots, first, target, place, sem):
    def one(i, carry):
        pltpu.make_async_copy(slots.at[place[first + i]], target.at[i], sem).start()
        return carry
    lax.fori_loop(0, target.shape[0], one, 0)


def fetch_wait(slots, target, sem):
    pltpu.make_async_copy(slots.at[pl.ds(0, target.shape[0])], target, sem).wait()


def send_panels(stage, first, mine, theirs, back, sem):
    half = mine.shape[0]

    def one(i, carry):
        slot = back[first + i]

        @pl.when(slot < half)
        def _():
            pltpu.make_async_copy(stage.at[i], mine.at[slot], sem).start()

        @pl.when(slot >= half)
        def _():
            pltpu.make_async_copy(stage.at[i], theirs.at[slot - half], sem).start()

        return carry

    lax.fori_loop(0, stage.shape[0], one, 0)


def send_wait(stage, mine, sem):
    pltpu.make_async_copy(stage, mine.at[pl.ds(0, stage.shape[0])], sem).wait()


def attn_fwd_kernel(limits, place, x_ref, slots_ref, small_ref, q_ref, k_ref, v_ref, c_ref, p_ref,
                    mixed_ref, zh_ref, rstd_ref, w_ref, w_sem):
    step = pl.program_id(0)
    groups = x_ref.shape[-1] // LANES // PAIRS_FWD
    seq, group = step // groups, step % groups
    d = x_ref.shape[-1]
    block = x_ref.shape[1]

    @pl.when(step == 0)
    def _():
        fetch_panels(slots_ref, 0, w_ref, place, w_sem)
        fetch_wait(slots_ref, w_ref, w_sem)

    @pl.when(group == 0)
    def _():
        x = x_ref[0]
        q = mm(x, rows_of(w_ref, 0, d)) + small_ref[4:5, :]
        q_ref[0] = (q.astype(BF).astype(F32) * 0.125).astype(BF)
        k_ref[0] = mm(x, rows_of(w_ref, d, d)).astype(BF)
        v_ref[0] = (mm(x, rows_of(w_ref, 2 * d, d)) + small_ref[5:6, :]).astype(BF)

    limit = limits[seq]
    key = lax.broadcasted_iota(jnp.int32, (block, block), 0)
    for n in range(PAIRS_FWD):
        lanes = pl.ds(pl.multiple_of((group * PAIRS_FWD + n) * LANES, LANES), LANES)
        qp, kp, vp = q_ref[0, :, lanes], k_ref[0, :, lanes], v_ref[0, :, lanes]
        vt = vp.T
        parts = []
        for half in range(2):
            km = jnp.where(lane_half(kp.shape, half), kp, jnp.zeros_like(kp))
            s = mm_nt(km, qp)
            s = jnp.where(key < limit, s, masked_score)
            top = jnp.max(s, axis=0, keepdims=True)
            e = jnp.exp(s - top)
            total = jnp.sum(e, axis=0, keepdims=True)
            p = (e * (1.0 / total)).astype(BF)
            p_ref[2 * n + half] = p
            parts.append(mm(vt[half * HEAD_DIM:(half + 1) * HEAD_DIM], p))
        ctx_t = jnp.concatenate(parts, axis=0)
        c_ref[0, :, lanes] = ctx_t.T.astype(BF)

    @pl.when(group == groups - 1)
    def _():
        u = x_ref[0].astype(F32) + mm(c_ref[0], rows_of(w_ref, 3 * d, d)) + small_ref[6:7, :]
        zh, rstd = normalize(u)
        zh_ref[0] = zh
        rstd_ref[0] = rstd
        mixed_ref[0] = (zh * small_ref[0:1, :] + small_ref[1:2, :]).astype(BF)


def attn_fwd(x, gathered, small, limits, place):
    seqs, block, d = x.shape
    pairs = d // LANES
    groups = pairs // PAIRS_FWD
    by_seq = lambda shape: pl.BlockSpec((1,) + shape, lambda i, lim, pr: (i // groups, 0, 0))
    whole = lambda a: pl.BlockSpec(a, lambda i, lim, pr: (0, 0), pipeline_mode=pl.Buffered(1))
    act = jax.ShapeDtypeStruct((seqs, block, d), BF)
    return pl.pallas_call(
        attn_fwd_kernel,
        grid_spec=pltpu.PrefetchScalarGridSpec(
            num_scalar_prefetch=2,
            grid=(seqs * groups,),
            in_specs=[by_seq((block, d)), ANY, whole(small.shape)],
            out_specs=[by_seq((block, d))] * 4
            + [pl.BlockSpec((2 * PAIRS_FWD, block, block), lambda i, lim, pr: (i, 0, 0))]
            + [by_seq((block, d)), by_seq((block, d)), by_seq((block, 1))],
            scratch_shapes=[pltpu.VMEM((4 * d // PANEL, PANEL, d), BF), pltpu.SemaphoreType.DMA],
        ),
        out_shape=[act, act, act, act,
                   jax.ShapeDtypeStruct((seqs * 2 * pairs, block, block), BF),
                   act,
                   jax.ShapeDtypeStruct((seqs, block, d), F32),
                   jax.ShapeDtypeStruct((seqs, block, 1), F32)],
        compiler_params=pltpu.CompilerParams(vmem_limit_bytes=56 << 20, dimension_semantics=("arbitrary",)),
        name="attn_fwd",
    )(limits, place, x, gathered, small)


ROWS = 512
PAIRS_FWD = 2
PAIRS_BWD = 1
CHUNK = 1024


def ffn_kernel(place, back, mixed_ref, go_ref, w_hbm, small_ref, bh_ref,
               out_ref, dmixed_ref, sums_ref, dbh_ref, mine, theirs,
               w1, w2, hid, gp, acc, df, dyb, stage, w_sem, s_sem):
    d = mixed_ref.shape[-1]
    tokens = mixed_ref.shape[0]
    ff = bh_ref.shape[1]
    chunks = ff // CHUNK
    tiles = tokens // ROWS
    panels = CHUNK // PANEL
    first1 = 4 * d // PANEL
    first2 = first1 + ff // PANEL

    def start(c, carry):
        fetch_panels(w_hbm, first1 + c * panels, w1.at[c], place, w_sem.at[0, c])
        fetch_panels(w_hbm, first2 + c * panels, w2.at[c], place, w_sem.at[1, c])
        return carry

    lax.fori_loop(0, chunks, start, 0)

    def up(c, carry):
        fetch_wait(w_hbm, w1.at[c], w_sem.at[0, c])
        fetch_wait(w_hbm, w2.at[c], w_sem.at[1, c])
        cols = pl.ds(pl.multiple_of(c * CHUNK, CHUNK), CHUNK)
        w1c, w2c = w1[c].reshape(CHUNK, d), w2[c].reshape(CHUNK, d)
        bias = bh_ref[0:1, cols]
        for r in range(tiles):
            rows = pl.ds(r * ROWS, ROWS)
            f = mm_nt(mixed_ref[rows, :], w1c) + bias
            half_erf = 0.5 * lax.erf(f * (1.0 / math.sqrt(2.0))) + 0.5
            h = (f * half_erf).astype(BF)
            hid[rows, cols] = h
            gp[rows, cols] = (half_erf + f * (jnp.exp(-0.5 * f * f) * (1.0 / math.sqrt(2.0 * math.pi)))).astype(BF)
            part = mm(h, w2c)
            acc[rows, :] = jnp.where(c == 0, part, acc[rows, :] + part)
        return carry

    lax.fori_loop(0, chunks, up, 0)

    sums_ref[...] = jnp.zeros_like(sums_ref)

    def middle(r, carry):
        rows = pl.ds(pl.multiple_of(r * ROWS, ROWS), ROWS)
        rr = mixed_ref[rows, :].astype(F32) + acc[rows, :] + small_ref[7:8, :]
        zh, rstd = normalize(rr)
        out_ref[rows, :] = (zh * small_ref[2:3, :] + small_ref[3:4, :]).astype(BF)
        e = go_ref[rows, :].astype(F32)
        dr = norm_back(zh, rstd, e * small_ref[2:3, :])
        dy = dr.astype(BF)
        dyb[rows, :] = dy
        acc[rows, :] = dr
        sums_ref[0:1, :] += jnp.sum(e * zh, axis=0, keepdims=True)
        sums_ref[1:2, :] += jnp.sum(e, axis=0, keepdims=True)
        sums_ref[2:3, :] += jnp.sum(dy.astype(F32), axis=0, keepdims=True)
        return carry

    lax.fori_loop(0, tiles, middle, 0)

    def down(c, carry):
        cols = pl.ds(pl.multiple_of(c * CHUNK, CHUNK), CHUNK)
        w1c, w2c = w1[c].reshape(CHUNK, d), w2[c].reshape(CHUNK, d)
        dbh = jnp.zeros((1, CHUNK), F32)
        for r in range(tiles):
            rows = pl.ds(r * ROWS, ROWS)
            dfr = (mm_nt(dyb[rows, :], w2c) * gp[rows, cols].astype(F32)).astype(BF)
            df[rows, :] = dfr
            dbh += jnp.sum(dfr.astype(F32), axis=0, keepdims=True)
            acc[rows, :] += mm(dfr, w1c)
        dbh_ref[0:1, cols] = dbh

        @pl.when(c > 0)
        def _():
            send_wait(stage.at[0], mine, s_sem.at[0])
            send_wait(stage.at[1], mine, s_sem.at[1])

        stage[0] = mm_tn(df[...], mixed_ref[...]).astype(BF).reshape(panels, PANEL, d)
        send_panels(stage.at[0], first1 + c * panels, mine, theirs, back, s_sem.at[0])
        stage[1] = mm_tn(hid[:, cols], dyb[...]).astype(BF).reshape(panels, PANEL, d)
        send_panels(stage.at[1], first2 + c * panels, mine, theirs, back, s_sem.at[1])
        return carry

    lax.fori_loop(0, chunks, down, 0)
    dmixed_ref[...] = acc[...].astype(BF)
    send_wait(stage.at[0], mine, s_sem.at[0])
    send_wait(stage.at[1], mine, s_sem.at[1])


def ffn(mixed, go, gathered, small, bh, place, back, half):
    tokens, d = mixed.shape
    ff = bh.shape[1]
    full = lambda shape: pl.BlockSpec(shape, lambda i, pr, bk: (0,) * len(shape))
    return pl.pallas_call(
        ffn_kernel,
        grid_spec=pltpu.PrefetchScalarGridSpec(
            num_scalar_prefetch=2,
            grid=(1,),
            in_specs=[full((tokens, d)), full((tokens, d)), ANY,
                      full(small.shape), full(bh.shape)],
            out_specs=[full((tokens, d)), full((tokens, d)), full((8, d)), full((1, ff)),
                       ANY, ANY],
            scratch_shapes=[
                pltpu.VMEM((ff // CHUNK, CHUNK // PANEL, PANEL, d), BF),
                pltpu.VMEM((ff // CHUNK, CHUNK // PANEL, PANEL, d), BF),
                pltpu.VMEM((tokens, ff), BF), pltpu.VMEM((tokens, ff), BF),
                pltpu.VMEM((tokens, d), F32), pltpu.VMEM((tokens, CHUNK), BF),
                pltpu.VMEM((tokens, d), BF), pltpu.VMEM((2, CHUNK // PANEL, PANEL, d), BF),
                pltpu.SemaphoreType.DMA((2, ff // CHUNK)), pltpu.SemaphoreType.DMA((2,)),
            ],
        ),
        out_shape=[jax.ShapeDtypeStruct((tokens, d), BF), jax.ShapeDtypeStruct((tokens, d), BF),
                   jax.ShapeDtypeStruct((8, d), F32), jax.ShapeDtypeStruct((1, ff), F32),
                   jax.ShapeDtypeStruct((half, PANEL, d), BF), jax.ShapeDtypeStruct((half, PANEL, d), BF)],
        compiler_params=pltpu.CompilerParams(vmem_limit_bytes=60 << 20, dimension_semantics=("arbitrary",)),
        name="ffn",
    )(place, back, mixed, go, gathered, small, bh)


def attn_bwd_kernel(limits, place, back, dmixed_ref, zh_ref, rstd_ref, x_ref, q_ref, k_ref, v_ref,
                    c_ref, p_ref, w_hbm, small_ref, mine_in, theirs_in,
                    gin_ref, sums_ref, mine, theirs,
                    dctx, dq, dk, dv, dw, stage, w_ref, s_sem, w_sem):
    step = pl.program_id(0)
    groups = x_ref.shape[-1] // LANES // PAIRS_BWD
    seq, group = step // groups, step % groups
    d = x_ref.shape[-1]
    block = x_ref.shape[1]
    tiles = block // ROWS

    @pl.when(step == 0)
    def _():
        fetch_panels(w_hbm, 0, w_ref, place, w_sem)
        dw[...] = jnp.zeros_like(dw)
        sums_ref[...] = jnp.zeros_like(sums_ref)
        fetch_wait(w_hbm, w_ref, w_sem)

    @pl.when(group == 0)
    def _():
        for r in range(tiles):
            rows = pl.ds(r * ROWS, ROWS)
            e = dmixed_ref[0, rows, :].astype(F32)
            zh = zh_ref[0, rows, :]
            du = norm_back(zh, rstd_ref[0, rows, :], e * small_ref[0:1, :])
            da = du.astype(BF)
            gin_ref[0, rows, :] = du
            sums_ref[0:1, :] += jnp.sum(e * zh, axis=0, keepdims=True)
            sums_ref[1:2, :] += jnp.sum(e, axis=0, keepdims=True)
            sums_ref[4:5, :] += jnp.sum(da.astype(F32), axis=0, keepdims=True)
            dctx[rows, :] = mm_nt(da, rows_of(w_ref, 3 * d, d)).astype(BF)
            dw[pl.ds(3 * d, d), :] += mm_tn(c_ref[0, rows, :], da)

    limit = limits[seq]
    key = lax.broadcasted_iota(jnp.int32, (block, block), 0)
    for n in range(PAIRS_BWD):
        lanes = pl.ds(pl.multiple_of((group * PAIRS_BWD + n) * LANES, LANES), LANES)
        qp, kp, vp, dcp = q_ref[0, :, lanes], k_ref[0, :, lanes], v_ref[0, :, lanes], dctx[:, lanes]
        kt = kp.T
        prod_t = (dcp.astype(F32) * c_ref[0, :, lanes].astype(F32)).T
        dqt, dks, dvs = [], [], []
        for half in range(2):
            vm = jnp.where(lane_half(vp.shape, half), vp, jnp.zeros_like(vp))
            dp = mm_nt(vm, dcp)
            delta = jnp.sum(prod_t[half * HEAD_DIM:(half + 1) * HEAD_DIM], axis=0, keepdims=True)
            p = p_ref[2 * n + half]
            ds = jnp.where(key < limit, p.astype(F32) * (dp - delta), 0.0).astype(BF)
            dqt.append(mm(kt[half * HEAD_DIM:(half + 1) * HEAD_DIM], ds))
            dks.append(mm(ds, qp))
            dvs.append(mm(p, dcp))
        low = lane_half(qp.shape, 0)
        dq[:, lanes] = (jnp.concatenate(dqt, axis=0) * 0.125).T.astype(BF)
        dk[:, lanes] = jnp.where(low, dks[0], dks[1]).astype(BF)
        dv[:, lanes] = jnp.where(low, dvs[0], dvs[1]).astype(BF)

    @pl.when(group == groups - 1)
    def _():
        x = x_ref[0]
        gin_ref[0] += (mm_nt(dq[...], rows_of(w_ref, 0, d)) + mm_nt(dk[...], rows_of(w_ref, d, d))
                       + mm_nt(dv[...], rows_of(w_ref, 2 * d, d)))
        dw[pl.ds(0, d), :] += mm_tn(x, dq[...])
        dw[pl.ds(d, d), :] += mm_tn(x, dk[...])
        dw[pl.ds(2 * d, d), :] += mm_tn(x, dv[...])
        sums_ref[2:3, :] += jnp.sum(dq[...].astype(F32), axis=0, keepdims=True)
        sums_ref[3:4, :] += jnp.sum(dv[...].astype(F32), axis=0, keepdims=True)

    @pl.when(step == pl.num_programs(0) - 1)
    def _():
        stage[...] = dw[...].astype(BF).reshape(stage.shape)
        send_panels(stage, 0, mine, theirs, back, s_sem)
        send_wait(stage, mine, s_sem)


def attn_bwd(dmixed, zh, rstd, x, q, k, v, c, p, gathered, small, limits, place, back, mine, theirs):
    seqs, block, d = x.shape
    pairs = d // LANES
    groups = pairs // PAIRS_BWD
    by_seq = lambda shape: pl.BlockSpec((1,) + shape, lambda i, lim, pr, bk: (i // groups, 0, 0))
    whole = lambda a: pl.BlockSpec(a, lambda i, lim, pr, bk: (0, 0), pipeline_mode=pl.Buffered(1))
    return pl.pallas_call(
        attn_bwd_kernel,
        grid_spec=pltpu.PrefetchScalarGridSpec(
            num_scalar_prefetch=3,
            grid=(seqs * groups,),
            in_specs=[by_seq((block, d)), by_seq((block, d)), by_seq((block, 1))]
            + [by_seq((block, d))] * 5
            + [pl.BlockSpec((2 * PAIRS_BWD, block, block), lambda i, lim, pr, bk: (i, 0, 0)),
               ANY, whole(small.shape), ANY, ANY],
            out_specs=[by_seq((block, d)), pl.BlockSpec((8, d), lambda i, lim, pr, bk: (0, 0)),
                       ANY, ANY],
            scratch_shapes=[pltpu.VMEM((block, d), BF)] * 4
            + [pltpu.VMEM((4 * d, d), F32), pltpu.VMEM((4 * d // PANEL, PANEL, d), BF),
               pltpu.VMEM((4 * d // PANEL, PANEL, d), BF), pltpu.SemaphoreType.DMA, pltpu.SemaphoreType.DMA],
        ),
        out_shape=[jax.ShapeDtypeStruct((seqs, block, d), F32), jax.ShapeDtypeStruct((8, d), F32),
                   jax.ShapeDtypeStruct(mine.shape, BF), jax.ShapeDtypeStruct(mine.shape, BF)],
        input_output_aliases={14: 2, 15: 3},
        compiler_params=pltpu.CompilerParams(vmem_limit_bytes=60 << 20, dimension_semantics=("arbitrary",)),
        name="attn_bwd",
    )(limits, place, back, dmixed, zh, rstd, x, q, k, v, c, p, gathered, small, mine, theirs)


RING_ROUNDS = 5
LINKS = ("x", "y", "u", "d")
NEW_BLOCK = {
    (0, 0, "x"): (1, 0, 0), (0, 0, "y"): (0, 1, 0), (0, 0, "d"): (0, 0, 1),
    (0, 1, "x"): (1, 0, 1), (0, 1, "y"): (1, 1, 0), (0, 1, "d"): (0, 0, 2),
    (0, 2, "x"): (1, 0, 2), (0, 2, "y"): (0, 1, 2), (0, 2, "d"): (0, 0, 3),
    (0, 3, "x"): (1, 0, 3), (0, 3, "y"): (0, 1, 3), (0, 3, "d"): (1, 1, 2),
    (0, 4, "x"): (1, 1, 3), (0, 4, "y"): (1, 1, 1), (0, 4, "d"): (0, 1, 1),
    (1, 0, "x"): (1, 0, 1), (1, 0, "y"): (0, 1, 1), (1, 0, "u"): (0, 0, 0), (1, 0, "d"): (0, 0, 2),
    (1, 1, "x"): (1, 0, 2), (1, 1, "y"): (0, 1, 2), (1, 1, "u"): (1, 0, 0), (1, 1, "d"): (0, 0, 3),
    (1, 2, "x"): (1, 1, 2), (1, 2, "y"): (0, 1, 3), (1, 2, "u"): (0, 1, 0), (1, 2, "d"): (1, 0, 3),
    (1, 3, "x"): (1, 1, 0), (1, 3, "y"): (1, 1, 3), (1, 3, "d"): (1, 1, 1),
}
DUMMY = 16


def neighbour(chip, link):
    if link == "x":
        return chip ^ 1
    if link == "y":
        return chip ^ 2
    if link == "u":
        return chip - 4 if chip >= 4 else None
    return chip + 4 if chip < 12 else None


def received_block(chip, turn, link):
    layer = chip >> 2
    if layer < 2:
        block = NEW_BLOCK.get((layer, turn, link))
        if block is None:
            return None
        return block[2] * 4 + ((chip & 3) ^ (block[1] * 2 + block[0]))
    block = NEW_BLOCK.get((3 - layer, turn, {"u": "d", "d": "u"}.get(link, link)))
    if block is None:
        return None
    return (3 - block[2]) * 4 + ((chip & 3) ^ (block[1] * 2 + block[0]))


def build_schedule():
    moves, columns = [], []
    held = [{chip: -1} for chip in range(16)]
    for turn in range(RING_ROUNDS):
        fresh = []
        for link in LINKS:
            pairs, takes, gives, given = [], [DUMMY] * 16, [DUMMY] * 16, {}
            for chip in range(16):
                block = received_block(chip, turn, link)
                if block is None:
                    continue
                source = neighbour(chip, link)
                pairs.append((source, chip))
                takes[chip] = block
                gives[source] = block
                given[source] = held[source][block]
                fresh.append((chip, block, len(moves)))
            if not pairs:
                continue
            sources = sorted(set(given.values()))
            which = [sources.index(given.get(chip, sources[0])) for chip in range(16)]
            moves.append((turn, link, tuple(pairs), tuple(sources)))
            columns += [takes, which, gives]
        for chip, block, move in fresh:
            held[chip][block] = move
    return moves, np.array(columns, np.int32).T


MOVES, TABLE = build_schedule()


def feeders(move):
    takes = [received_block(chip, MOVES[move][0], MOVES[move][1]) for chip in range(16)]
    return feeding(takes, MOVES[move][0])


def feeding(blocks, turn):
    found = []
    for later, (after, link, pairs, _) in enumerate(MOVES):
        if after <= turn:
            continue
        chips = [
            source for source, target in pairs
            if blocks[source] is not None and received_block(target, after, link) == blocks[source]
        ]
        if chips:
            found.append((later, tuple(chips)))
    return found


def build_feeds():
    feeds, columns = [], []
    for move in range(len(MOVES) + 1):
        found = feeders(move) if move < len(MOVES) else feeding(list(range(16)), -1)
        feeds.append([(later, len(columns) + i) for i, (later, _) in enumerate(found)])
        columns += [[int(chip in chips) for chip in range(16)] for _, chips in found]
    return feeds, np.array(columns, np.int32).T


FEEDS, FEED_TABLE = build_feeds()


def both_kernel(mine, pair, out):
    out[...] = mine[...] + pair[...]


def add_cores(mine, pair):
    shape = (1,) + mine.shape[1:]
    block = pl.BlockSpec(shape, lambda i: (i, 0, 0, 0))
    return pl.pallas_call(
        both_kernel, grid=(mine.shape[0],), in_specs=[block, block], out_specs=block,
        out_shape=jax.ShapeDtypeStruct(mine.shape, BF),
        cost_estimate=pl.CostEstimate(flops=0, bytes_accessed=6 * mine.size, transcendentals=0),
        compiler_params=pltpu.CompilerParams(vmem_limit_bytes=8 << 20),
        name="add_cores",
    )(mine, pair)


def add_kernel(flags, row, feed, own, *refs):
    out, acc = refs[-2], refs[-1]

    def slot(r, carry):
        acc[...] = own[0, r].astype(F32)
        for ref, column in zip(refs[:-2], flags):
            @pl.when(feed[column] == 1)
            def _():
                acc[...] += ref[r].astype(F32)
        out[r] = acc[...].astype(out.dtype)
        return carry

    lax.fori_loop(0, out.shape[0], slot, 0)


def add_block(row, feed, block_column, sums, arrays, flags, dtype):
    slots = sums.shape[1]
    shape = sums.shape[1:]
    pieces = 2 if slots % 2 == 0 else 1
    piece = (slots // pieces,) + shape[1:]
    by_block = pl.BlockSpec((1,) + piece, lambda i, rw, fd: (rw[block_column], i, 0, 0))
    plain = pl.BlockSpec(piece, lambda i, rw, fd: (i, 0, 0))
    return pl.pallas_call(
        partial(add_kernel, tuple(flags)),
        grid_spec=pltpu.PrefetchScalarGridSpec(
            num_scalar_prefetch=2, grid=(pieces,),
            in_specs=[by_block] + [plain] * len(arrays), out_specs=plain,
            scratch_shapes=[pltpu.VMEM(piece[1:], F32)]),
        out_shape=jax.ShapeDtypeStruct(shape, dtype),
        cost_estimate=pl.CostEstimate(
            flops=0, bytes_accessed=2 * sums[0].size * (2 + len(arrays)), transcendentals=0),
        compiler_params=pltpu.CompilerParams(vmem_limit_bytes=12 << 20),
        name="add_block",
    )(row, feed, sums, *arrays)


def partners():
    size = lax.axis_size("batch")
    steps, bit = [], 1
    while bit < size:
        steps.append(("batch", tuple((i, i ^ bit) for i in range(size))))
        bit *= 2
    return steps + [("seq", SWAP)]


def reduce_slots(mine, theirs, small):
    me = lax.axis_index("batch")
    takes = jnp.asarray(TABLE)[me][0::3]
    row = jnp.concatenate([jnp.where(takes == DUMMY, 0, takes), jnp.stack([me])])
    feed = jnp.asarray(FEED_TABLE)[me]
    pair = lax.ppermute(theirs, "seq", SWAP)
    mine = mine.reshape((16, -1) + mine.shape[1:])
    sums = add_cores(mine, pair.reshape(mine.shape))
    steps = partners()
    early = small
    for step in (steps.pop(-2), steps.pop(-2)):
        early = early + lax.ppermute(early, *step)
    small = early
    before = []
    arrived, ready = {}, lax.optimization_barrier((row, early))[0]
    for turn in reversed(range(RING_ROUNDS)):
        gives = []
        now = [i for i, move in enumerate(MOVES) if move[0] == turn]
        for i in now:
            give = add_block(ready, feed, i, sums, [arrived[m] for m, _ in FEEDS[i]],
                             [column for _, column in FEEDS[i]], BF)
            gives.append(give)
            back = tuple((target, source) for source, target in MOVES[i][2])
            arrived[i] = lax.ppermute(give, "batch", back)
        late = [arrived[i] for i in before]
        ready, small, *late = lax.optimization_barrier((row, small, *late, *gives))
        arrived.update(zip(before, late))
        before = now
        if steps:
            small = small + lax.ppermute(small, *steps.pop(0))
    for step in steps:
        small = small + lax.ppermute(small, *step)
    last = FEEDS[len(MOVES)]
    total = add_block(row, feed, len(MOVES), sums, [arrived[m] for m, _ in last],
                      [column for _, column in last], F32)
    return total, small


def slot_table(owners, capacity):
    panel_index = jnp.arange(owners.shape[0], dtype=jnp.int32)
    same_owner = (owners[:, None] == owners[None, :]) & (
        panel_index[None, :] < panel_index[:, None]
    )
    rank_within = jnp.sum(same_owner.astype(jnp.int32), axis=1)
    return owners * capacity + rank_within


def adam_update(weight, first_old, second_old, grad_now, step_count):
    step_float = step_count[0].astype(jnp.float32)
    first_new = beta_first * first_old + (1.0 - beta_first) * grad_now
    second_new = beta_second * second_old + (1.0 - beta_second) * grad_now * grad_now
    first_hat = first_new / (1.0 - jnp.power(beta_first, step_float))
    second_hat = second_new / (1.0 - jnp.power(beta_second, step_float))
    weight_new = weight - learn_rate * (
        first_hat / (jnp.sqrt(second_hat) + adam_eps) + decay_rate * weight
    )
    return (weight_new, first_new, second_new)


def local(
    tokens,
    grad_out,
    lengths,
    owners,
    weight_slots,
    first_slots,
    second_slots,
    small_params,
    small_first,
    small_second,
    step_count,
):
    capacity = weight_slots.shape[0]
    block_rows, features = tokens.shape[1:]
    slot_of = slot_table(owners, capacity)
    devices = lax.axis_size("seq") * lax.axis_size("batch")
    device = lax.axis_index("seq") * lax.axis_size("batch") + lax.axis_index("batch")
    limits = lengths - lax.axis_index("seq") * block_rows
    core = lax.axis_index("seq")
    batch = lax.axis_size("batch")
    half = batch * capacity
    owner_core = (owners >= batch).astype(jnp.int32)
    back = slot_of - owner_core * half + jnp.where(owner_core == core, 0, half)
    gathered = lax.all_gather(weight_slots.astype(BF), ("seq", "batch"), axis=0, tiled=True)
    q, k, v, ctx, probs, mixed, zh, rstd = attn_fwd(tokens, gathered, small_params, limits, slot_of)
    bias_hidden = small_params[8:].reshape(1, -1)
    layer_out, d_mixed, sums_ffn, d_bias, mine, theirs = ffn(
        mixed.reshape(-1, features), grad_out.reshape(-1, features), gathered, small_params,
        bias_hidden, slot_of, back, half)
    grad_in, sums_attn, mine, theirs = attn_bwd(
        d_mixed.reshape(tokens.shape), zh, rstd, tokens, q, k, v, ctx, probs, gathered,
        small_params, limits, slot_of, back, mine, theirs)
    small_local = jnp.concatenate(
        [sums_attn[0:2], sums_ffn[0:2], sums_attn[2:5], sums_ffn[2:3],
         d_bias.reshape(-1, features)], axis=0)
    if batch == 16 and lax.axis_size("seq") == 2:
        grad_slots, small_grad = reduce_slots(mine, theirs, small_local)
    else:
        both = jnp.where(core == 0, jnp.stack([mine, theirs]), jnp.stack([theirs, mine]))
        grad_slots = lax.psum_scatter(
            both.reshape((-1,) + mine.shape[1:]), ("seq", "batch"), scatter_dimension=0,
            tiled=True).astype(jnp.float32)
        small_grad = small_local
        for step in partners():
            small_grad = small_grad + lax.ppermute(small_grad, *step)
    held = jnp.sum((owners == device).astype(jnp.int32))
    used = jnp.arange(capacity, dtype=jnp.int32) < held
    grad_slots = jnp.where(used[:, None, None], grad_slots, 0.0)
    new_slots, new_first_slots, new_second_slots = adam_update(
        weight_slots, first_slots, second_slots, grad_slots, step_count
    )
    new_small, new_small_first, new_small_second = adam_update(
        small_params, small_first, small_second, small_grad, step_count
    )
    return (
        layer_out.reshape(tokens.shape),
        grad_in,
        grad_slots,
        new_slots,
        new_first_slots,
        new_second_slots,
        small_grad,
        new_small,
        new_small_first,
        new_small_second,
    )


def solution(mesh):
    in_specs = (
        P("batch", "seq", None),
        P("batch", "seq", None),
        P("batch"),
        P(),
        P(("seq", "batch"), None, None),
        P(("seq", "batch"), None, None),
        P(("seq", "batch"), None, None),
        P(),
        P(),
        P(),
        P(),
    )
    out_specs = (
        P("batch", "seq", None),
        P("batch", "seq", None),
        P(("seq", "batch"), None, None),
        P(("seq", "batch"), None, None),
        P(("seq", "batch"), None, None),
        P(("seq", "batch"), None, None),
        P(),
        P(),
        P(),
        P(),
    )
    return jax.shard_map(local, mesh=mesh, in_specs=in_specs, out_specs=out_specs, check_vma=False)
```

```python
from functools import partial
import math

import jax
import jax.numpy as jnp
import numpy as np
from jax import lax
from jax.experimental import pallas as pl
from jax.experimental.pallas import tpu as pltpu
from jax.sharding import PartitionSpec as P

beta_first = 0.9
beta_second = 0.999
adam_eps = 1e-08
learn_rate = 0.2
decay_rate = 0.01
SWAP = ((0, 1), (1, 0))

HEAD_DIM = 64
PANEL = 32
norm_eps = 1e-06
masked_score = -30.0
LANES = 128
BF = jnp.bfloat16
F32 = jnp.float32
ANY = pl.BlockSpec(memory_space=pl.ANY)


def mm(a, b):
    return lax.dot_general(a, b, (((1,), (0,)), ((), ())), preferred_element_type=F32)


def mm_nt(a, b):
    return lax.dot_general(a, b, (((1,), (1,)), ((), ())), preferred_element_type=F32)


def mm_tn(a, b):
    return lax.dot_general(a, b, (((0,), (0,)), ((), ())), preferred_element_type=F32)


def normalize(z):
    centre = z - jnp.mean(z, axis=-1, keepdims=True)
    rstd = lax.rsqrt(jnp.mean(centre * centre, axis=-1, keepdims=True) + norm_eps)
    return centre * rstd, rstd


def norm_back(zh, rstd, t):
    mean_t = jnp.mean(t, axis=-1, keepdims=True)
    mean_tz = jnp.mean(t * zh, axis=-1, keepdims=True)
    return (t - mean_t - zh * mean_tz) * rstd


def lane_half(shape, half):
    lane = lax.broadcasted_iota(jnp.int32, shape, len(shape) - 1)
    return (lane < HEAD_DIM) if half == 0 else (lane >= HEAD_DIM)


def rows_of(panels, start, count):
    return panels[start // PANEL:(start + count) // PANEL].reshape(count, panels.shape[-1])


def fetch_panels(slots, first, target, place, sem):
    def one(i, carry):
        pltpu.make_async_copy(slots.at[place[first + i]], target.at[i], sem).start()
        return carry
    lax.fori_loop(0, target.shape[0], one, 0)


def fetch_wait(slots, target, sem):
    pltpu.make_async_copy(slots.at[pl.ds(0, target.shape[0])], target, sem).wait()


def send_panels(stage, first, mine, theirs, back, sem):
    half = mine.shape[0]

    def one(i, carry):
        slot = back[first + i]

        @pl.when(slot < half)
        def _():
            pltpu.make_async_copy(stage.at[i], mine.at[slot], sem).start()

        @pl.when(slot >= half)
        def _():
            pltpu.make_async_copy(stage.at[i], theirs.at[slot - half], sem).start()

        return carry

    lax.fori_loop(0, stage.shape[0], one, 0)


def send_wait(stage, mine, sem):
    pltpu.make_async_copy(stage, mine.at[pl.ds(0, stage.shape[0])], sem).wait()


def attn_fwd_kernel(limits, place, x_ref, slots_ref, small_ref, q_ref, k_ref, v_ref, c_ref, p_ref,
                    mixed_ref, zh_ref, rstd_ref, w_ref, w_sem):
    step = pl.program_id(0)
    groups = x_ref.shape[-1] // LANES // PAIRS_FWD
    seq, group = step // groups, step % groups
    d = x_ref.shape[-1]
    block = x_ref.shape[1]

    @pl.when(step == 0)
    def _():
        fetch_panels(slots_ref, 0, w_ref, place, w_sem)
        fetch_wait(slots_ref, w_ref, w_sem)

    @pl.when(group == 0)
    def _():
        x = x_ref[0]
        q = mm(x, rows_of(w_ref, 0, d)) + small_ref[4:5, :]
        q_ref[0] = (q.astype(BF).astype(F32) * 0.125).astype(BF)
        k_ref[0] = mm(x, rows_of(w_ref, d, d)).astype(BF)
        v_ref[0] = (mm(x, rows_of(w_ref, 2 * d, d)) + small_ref[5:6, :]).astype(BF)

    limit = limits[seq]
    key = lax.broadcasted_iota(jnp.int32, (block, block), 0)
    for n in range(PAIRS_FWD):
        lanes = pl.ds(pl.multiple_of((group * PAIRS_FWD + n) * LANES, LANES), LANES)
        qp, kp, vp = q_ref[0, :, lanes], k_ref[0, :, lanes], v_ref[0, :, lanes]
        vt = vp.T
        parts = []
        for half in range(2):
            km = jnp.where(lane_half(kp.shape, half), kp, jnp.zeros_like(kp))
            s = mm_nt(km, qp)
            s = jnp.where(key < limit, s, masked_score)
            top = jnp.max(s, axis=0, keepdims=True)
            e = jnp.exp(s - top)
            total = jnp.sum(e, axis=0, keepdims=True)
            p = (e * (1.0 / total)).astype(BF)
            p_ref[2 * n + half] = p
            parts.append(mm(vt[half * HEAD_DIM:(half + 1) * HEAD_DIM], p))
        ctx_t = jnp.concatenate(parts, axis=0)
        c_ref[0, :, lanes] = ctx_t.T.astype(BF)

    @pl.when(group == groups - 1)
    def _():
        u = x_ref[0].astype(F32) + mm(c_ref[0], rows_of(w_ref, 3 * d, d)) + small_ref[6:7, :]
        zh, rstd = normalize(u)
        zh_ref[0] = zh
        rstd_ref[0] = rstd
        mixed_ref[0] = (zh * small_ref[0:1, :] + small_ref[1:2, :]).astype(BF)


def attn_fwd(x, gathered, small, limits, place):
    seqs, block, d = x.shape
    pairs = d // LANES
    groups = pairs // PAIRS_FWD
    by_seq = lambda shape: pl.BlockSpec((1,) + shape, lambda i, lim, pr: (i // groups, 0, 0))
    whole = lambda a: pl.BlockSpec(a, lambda i, lim, pr: (0, 0), pipeline_mode=pl.Buffered(1))
    act = jax.ShapeDtypeStruct((seqs, block, d), BF)
    return pl.pallas_call(
        attn_fwd_kernel,
        grid_spec=pltpu.PrefetchScalarGridSpec(
            num_scalar_prefetch=2,
            grid=(seqs * groups,),
            in_specs=[by_seq((block, d)), ANY, whole(small.shape)],
            out_specs=[by_seq((block, d))] * 4
            + [pl.BlockSpec((2 * PAIRS_FWD, block, block), lambda i, lim, pr: (i, 0, 0))]
            + [by_seq((block, d)), by_seq((block, d)), by_seq((block, 1))],
            scratch_shapes=[pltpu.VMEM((4 * d // PANEL, PANEL, d), BF), pltpu.SemaphoreType.DMA],
        ),
        out_shape=[act, act, act, act,
                   jax.ShapeDtypeStruct((seqs * 2 * pairs, block, block), BF),
                   act,
                   jax.ShapeDtypeStruct((seqs, block, d), F32),
                   jax.ShapeDtypeStruct((seqs, block, 1), F32)],
        compiler_params=pltpu.CompilerParams(vmem_limit_bytes=56 << 20, dimension_semantics=("arbitrary",)),
        name="attn_fwd",
    )(limits, place, x, gathered, small)


ROWS = 512
PAIRS_FWD = 2
PAIRS_BWD = 1
CHUNK = 1024


def ffn_kernel(place, back, mixed_ref, go_ref, w_hbm, small_ref, bh_ref,
               out_ref, dmixed_ref, sums_ref, dbh_ref, mine, theirs,
               w1, w2, hid, gp, acc, df, dyb, stage, w_sem, s_sem):
    d = mixed_ref.shape[-1]
    tokens = mixed_ref.shape[0]
    ff = bh_ref.shape[1]
    chunks = ff // CHUNK
    tiles = tokens // ROWS
    panels = CHUNK // PANEL
    first1 = 4 * d // PANEL
    first2 = first1 + ff // PANEL

    def start(c, carry):
        fetch_panels(w_hbm, first1 + c * panels, w1.at[c], place, w_sem.at[0, c])
        fetch_panels(w_hbm, first2 + c * panels, w2.at[c], place, w_sem.at[1, c])
        return carry

    lax.fori_loop(0, chunks, start, 0)

    def up(c, carry):
        fetch_wait(w_hbm, w1.at[c], w_sem.at[0, c])
        fetch_wait(w_hbm, w2.at[c], w_sem.at[1, c])
        cols = pl.ds(pl.multiple_of(c * CHUNK, CHUNK), CHUNK)
        w1c, w2c = w1[c].reshape(CHUNK, d), w2[c].reshape(CHUNK, d)
        bias = bh_ref[0:1, cols]
        for r in range(tiles):
            rows = pl.ds(r * ROWS, ROWS)
            f = mm_nt(mixed_ref[rows, :], w1c) + bias
            half_erf = 0.5 * lax.erf(f * (1.0 / math.sqrt(2.0))) + 0.5
            h = (f * half_erf).astype(BF)
            hid[rows, cols] = h
            gp[rows, cols] = (half_erf + f * (jnp.exp(-0.5 * f * f) * (1.0 / math.sqrt(2.0 * math.pi)))).astype(BF)
            part = mm(h, w2c)
            acc[rows, :] = jnp.where(c == 0, part, acc[rows, :] + part)
        return carry

    lax.fori_loop(0, chunks, up, 0)

    sums_ref[...] = jnp.zeros_like(sums_ref)

    def middle(r, carry):
        rows = pl.ds(pl.multiple_of(r * ROWS, ROWS), ROWS)
        rr = mixed_ref[rows, :].astype(F32) + acc[rows, :] + small_ref[7:8, :]
        zh, rstd = normalize(rr)
        out_ref[rows, :] = (zh * small_ref[2:3, :] + small_ref[3:4, :]).astype(BF)
        e = go_ref[rows, :].astype(F32)
        dr = norm_back(zh, rstd, e * small_ref[2:3, :])
        dy = dr.astype(BF)
        dyb[rows, :] = dy
        acc[rows, :] = dr
        sums_ref[0:1, :] += jnp.sum(e * zh, axis=0, keepdims=True)
        sums_ref[1:2, :] += jnp.sum(e, axis=0, keepdims=True)
        sums_ref[2:3, :] += jnp.sum(dy.astype(F32), axis=0, keepdims=True)
        return carry

    lax.fori_loop(0, tiles, middle, 0)

    def down(c, carry):
        cols = pl.ds(pl.multiple_of(c * CHUNK, CHUNK), CHUNK)
        w1c, w2c = w1[c].reshape(CHUNK, d), w2[c].reshape(CHUNK, d)
        dbh = jnp.zeros((1, CHUNK), F32)
        for r in range(tiles):
            rows = pl.ds(r * ROWS, ROWS)
            dfr = (mm_nt(dyb[rows, :], w2c) * gp[rows, cols].astype(F32)).astype(BF)
            df[rows, :] = dfr
            dbh += jnp.sum(dfr.astype(F32), axis=0, keepdims=True)
            acc[rows, :] += mm(dfr, w1c)
        dbh_ref[0:1, cols] = dbh

        @pl.when(c > 0)
        def _():
            send_wait(stage.at[0], mine, s_sem.at[0])
            send_wait(stage.at[1], mine, s_sem.at[1])

        stage[0] = mm_tn(df[...], mixed_ref[...]).astype(BF).reshape(panels, PANEL, d)
        send_panels(stage.at[0], first1 + c * panels, mine, theirs, back, s_sem.at[0])
        stage[1] = mm_tn(hid[:, cols], dyb[...]).astype(BF).reshape(panels, PANEL, d)
        send_panels(stage.at[1], first2 + c * panels, mine, theirs, back, s_sem.at[1])
        return carry

    lax.fori_loop(0, chunks, down, 0)
    dmixed_ref[...] = acc[...].astype(BF)
    send_wait(stage.at[0], mine, s_sem.at[0])
    send_wait(stage.at[1], mine, s_sem.at[1])


def ffn(mixed, go, gathered, small, bh, place, back, half):
    tokens, d = mixed.shape
    ff = bh.shape[1]
    full = lambda shape: pl.BlockSpec(shape, lambda i, pr, bk: (0,) * len(shape))
    return pl.pallas_call(
        ffn_kernel,
        grid_spec=pltpu.PrefetchScalarGridSpec(
            num_scalar_prefetch=2,
            grid=(1,),
            in_specs=[full((tokens, d)), full((tokens, d)), ANY,
                      full(small.shape), full(bh.shape)],
            out_specs=[full((tokens, d)), full((tokens, d)), full((8, d)), full((1, ff)),
                       ANY, ANY],
            scratch_shapes=[
                pltpu.VMEM((ff // CHUNK, CHUNK // PANEL, PANEL, d), BF),
                pltpu.VMEM((ff // CHUNK, CHUNK // PANEL, PANEL, d), BF),
                pltpu.VMEM((tokens, ff), BF), pltpu.VMEM((tokens, ff), BF),
                pltpu.VMEM((tokens, d), F32), pltpu.VMEM((tokens, CHUNK), BF),
                pltpu.VMEM((tokens, d), BF), pltpu.VMEM((2, CHUNK // PANEL, PANEL, d), BF),
                pltpu.SemaphoreType.DMA((2, ff // CHUNK)), pltpu.SemaphoreType.DMA((2,)),
            ],
        ),
        out_shape=[jax.ShapeDtypeStruct((tokens, d), BF), jax.ShapeDtypeStruct((tokens, d), BF),
                   jax.ShapeDtypeStruct((8, d), F32), jax.ShapeDtypeStruct((1, ff), F32),
                   jax.ShapeDtypeStruct((half, PANEL, d), BF), jax.ShapeDtypeStruct((half, PANEL, d), BF)],
        compiler_params=pltpu.CompilerParams(vmem_limit_bytes=60 << 20, dimension_semantics=("arbitrary",)),
        name="ffn",
    )(place, back, mixed, go, gathered, small, bh)


def attn_bwd_kernel(limits, place, back, dmixed_ref, zh_ref, rstd_ref, x_ref, q_ref, k_ref, v_ref,
                    c_ref, p_ref, w_hbm, small_ref, mine_in, theirs_in,
                    gin_ref, sums_ref, mine, theirs,
                    dctx, dq, dk, dv, dw, stage, w_ref, s_sem, w_sem):
    step = pl.program_id(0)
    groups = x_ref.shape[-1] // LANES // PAIRS_BWD
    seq, group = step // groups, step % groups
    d = x_ref.shape[-1]
    block = x_ref.shape[1]
    tiles = block // ROWS

    @pl.when(step == 0)
    def _():
        fetch_panels(w_hbm, 0, w_ref, place, w_sem)
        dw[...] = jnp.zeros_like(dw)
        sums_ref[...] = jnp.zeros_like(sums_ref)
        fetch_wait(w_hbm, w_ref, w_sem)

    @pl.when(group == 0)
    def _():
        for r in range(tiles):
            rows = pl.ds(r * ROWS, ROWS)
            e = dmixed_ref[0, rows, :].astype(F32)
            zh = zh_ref[0, rows, :]
            du = norm_back(zh, rstd_ref[0, rows, :], e * small_ref[0:1, :])
            da = du.astype(BF)
            gin_ref[0, rows, :] = du
            sums_ref[0:1, :] += jnp.sum(e * zh, axis=0, keepdims=True)
            sums_ref[1:2, :] += jnp.sum(e, axis=0, keepdims=True)
            sums_ref[4:5, :] += jnp.sum(da.astype(F32), axis=0, keepdims=True)
            dctx[rows, :] = mm_nt(da, rows_of(w_ref, 3 * d, d)).astype(BF)
            dw[pl.ds(3 * d, d), :] += mm_tn(c_ref[0, rows, :], da)

    limit = limits[seq]
    key = lax.broadcasted_iota(jnp.int32, (block, block), 0)
    for n in range(PAIRS_BWD):
        lanes = pl.ds(pl.multiple_of((group * PAIRS_BWD + n) * LANES, LANES), LANES)
        qp, kp, vp, dcp = q_ref[0, :, lanes], k_ref[0, :, lanes], v_ref[0, :, lanes], dctx[:, lanes]
        kt = kp.T
        prod_t = (dcp.astype(F32) * c_ref[0, :, lanes].astype(F32)).T
        dqt, dks, dvs = [], [], []
        for half in range(2):
            vm = jnp.where(lane_half(vp.shape, half), vp, jnp.zeros_like(vp))
            dp = mm_nt(vm, dcp)
            delta = jnp.sum(prod_t[half * HEAD_DIM:(half + 1) * HEAD_DIM], axis=0, keepdims=True)
            p = p_ref[2 * n + half]
            ds = jnp.where(key < limit, p.astype(F32) * (dp - delta), 0.0).astype(BF)
            dqt.append(mm(kt[half * HEAD_DIM:(half + 1) * HEAD_DIM], ds))
            dks.append(mm(ds, qp))
            dvs.append(mm(p, dcp))
        low = lane_half(qp.shape, 0)
        dq[:, lanes] = (jnp.concatenate(dqt, axis=0) * 0.125).T.astype(BF)
        dk[:, lanes] = jnp.where(low, dks[0], dks[1]).astype(BF)
        dv[:, lanes] = jnp.where(low, dvs[0], dvs[1]).astype(BF)

    @pl.when(group == groups - 1)
    def _():
        x = x_ref[0]
        gin_ref[0] += (mm_nt(dq[...], rows_of(w_ref, 0, d)) + mm_nt(dk[...], rows_of(w_ref, d, d))
                       + mm_nt(dv[...], rows_of(w_ref, 2 * d, d)))
        dw[pl.ds(0, d), :] += mm_tn(x, dq[...])
        dw[pl.ds(d, d), :] += mm_tn(x, dk[...])
        dw[pl.ds(2 * d, d), :] += mm_tn(x, dv[...])
        sums_ref[2:3, :] += jnp.sum(dq[...].astype(F32), axis=0, keepdims=True)
        sums_ref[3:4, :] += jnp.sum(dv[...].astype(F32), axis=0, keepdims=True)

    @pl.when(step == pl.num_programs(0) - 1)
    def _():
        stage[...] = dw[...].astype(BF).reshape(stage.shape)
        send_panels(stage, 0, mine, theirs, back, s_sem)
        send_wait(stage, mine, s_sem)


def attn_bwd(dmixed, zh, rstd, x, q, k, v, c, p, gathered, small, limits, place, back, mine, theirs):
    seqs, block, d = x.shape
    pairs = d // LANES
    groups = pairs // PAIRS_BWD
    by_seq = lambda shape: pl.BlockSpec((1,) + shape, lambda i, lim, pr, bk: (i // groups, 0, 0))
    whole = lambda a: pl.BlockSpec(a, lambda i, lim, pr, bk: (0, 0), pipeline_mode=pl.Buffered(1))
    return pl.pallas_call(
        attn_bwd_kernel,
        grid_spec=pltpu.PrefetchScalarGridSpec(
            num_scalar_prefetch=3,
            grid=(seqs * groups,),
            in_specs=[by_seq((block, d)), by_seq((block, d)), by_seq((block, 1))]
            + [by_seq((block, d))] * 5
            + [pl.BlockSpec((2 * PAIRS_BWD, block, block), lambda i, lim, pr, bk: (i, 0, 0)),
               ANY, whole(small.shape), ANY, ANY],
            out_specs=[by_seq((block, d)), pl.BlockSpec((8, d), lambda i, lim, pr, bk: (0, 0)),
                       ANY, ANY],
            scratch_shapes=[pltpu.VMEM((block, d), BF)] * 4
            + [pltpu.VMEM((4 * d, d), F32), pltpu.VMEM((4 * d // PANEL, PANEL, d), BF),
               pltpu.VMEM((4 * d // PANEL, PANEL, d), BF), pltpu.SemaphoreType.DMA, pltpu.SemaphoreType.DMA],
        ),
        out_shape=[jax.ShapeDtypeStruct((seqs, block, d), F32), jax.ShapeDtypeStruct((8, d), F32),
                   jax.ShapeDtypeStruct(mine.shape, BF), jax.ShapeDtypeStruct(mine.shape, BF)],
        input_output_aliases={14: 2, 15: 3},
        compiler_params=pltpu.CompilerParams(vmem_limit_bytes=60 << 20, dimension_semantics=("arbitrary",)),
        name="attn_bwd",
    )(limits, place, back, dmixed, zh, rstd, x, q, k, v, c, p, gathered, small, mine, theirs)


RING_ROUNDS = 5
LINKS = ("x", "y", "u", "d")
NEW_BLOCK = {
    (0, 0, "x"): (1, 0, 0), (0, 0, "y"): (0, 1, 0), (0, 0, "d"): (0, 0, 1),
    (0, 1, "x"): (1, 0, 1), (0, 1, "y"): (1, 1, 0), (0, 1, "d"): (0, 0, 2),
    (0, 2, "x"): (1, 0, 2), (0, 2, "y"): (0, 1, 2), (0, 2, "d"): (0, 0, 3),
    (0, 3, "x"): (1, 0, 3), (0, 3, "y"): (0, 1, 3), (0, 3, "d"): (1, 1, 2),
    (0, 4, "x"): (1, 1, 3), (0, 4, "y"): (1, 1, 1), (0, 4, "d"): (0, 1, 1),
    (1, 0, "x"): (1, 0, 1), (1, 0, "y"): (0, 1, 1), (1, 0, "u"): (0, 0, 0), (1, 0, "d"): (0, 0, 2),
    (1, 1, "x"): (1, 0, 2), (1, 1, "y"): (0, 1, 2), (1, 1, "u"): (1, 0, 0), (1, 1, "d"): (0, 0, 3),
    (1, 2, "x"): (1, 1, 2), (1, 2, "y"): (0, 1, 3), (1, 2, "u"): (0, 1, 0), (1, 2, "d"): (1, 0, 3),
    (1, 3, "x"): (1, 1, 0), (1, 3, "y"): (1, 1, 3), (1, 3, "d"): (1, 1, 1),
}
DUMMY = 16


def neighbour(chip, link):
    if link == "x":
        return chip ^ 1
    if link == "y":
        return chip ^ 2
    if link == "u":
        return chip - 4 if chip >= 4 else None
    return chip + 4 if chip < 12 else None


def received_block(chip, turn, link):
    layer = chip >> 2
    if layer < 2:
        block = NEW_BLOCK.get((layer, turn, link))
        if block is None:
            return None
        return block[2] * 4 + ((chip & 3) ^ (block[1] * 2 + block[0]))
    block = NEW_BLOCK.get((3 - layer, turn, {"u": "d", "d": "u"}.get(link, link)))
    if block is None:
        return None
    return (3 - block[2]) * 4 + ((chip & 3) ^ (block[1] * 2 + block[0]))


def build_schedule():
    moves, columns = [], []
    held = [{chip: -1} for chip in range(16)]
    for turn in range(RING_ROUNDS):
        fresh = []
        for link in LINKS:
            pairs, takes, gives, given = [], [DUMMY] * 16, [DUMMY] * 16, {}
            for chip in range(16):
                block = received_block(chip, turn, link)
                if block is None:
                    continue
                source = neighbour(chip, link)
                pairs.append((source, chip))
                takes[chip] = block
                gives[source] = block
                given[source] = held[source][block]
                fresh.append((chip, block, len(moves)))
            if not pairs:
                continue
            sources = sorted(set(given.values()))
            which = [sources.index(given.get(chip, sources[0])) for chip in range(16)]
            moves.append((turn, link, tuple(pairs), tuple(sources)))
            columns += [takes, which, gives]
        for chip, block, move in fresh:
            held[chip][block] = move
    return moves, np.array(columns, np.int32).T


MOVES, TABLE = build_schedule()


def feeders(move):
    takes = [received_block(chip, MOVES[move][0], MOVES[move][1]) for chip in range(16)]
    return feeding(takes, MOVES[move][0])


def feeding(blocks, turn):
    found = []
    for later, (after, link, pairs, _) in enumerate(MOVES):
        if after <= turn:
            continue
        chips = [
            source for source, target in pairs
            if blocks[source] is not None and received_block(target, after, link) == blocks[source]
        ]
        if chips:
            found.append((later, tuple(chips)))
    return found


def build_feeds():
    feeds, columns = [], []
    for move in range(len(MOVES) + 1):
        found = feeders(move) if move < len(MOVES) else feeding(list(range(16)), -1)
        feeds.append([(later, len(columns) + i) for i, (later, _) in enumerate(found)])
        columns += [[int(chip in chips) for chip in range(16)] for _, chips in found]
    return feeds, np.array(columns, np.int32).T


FEEDS, FEED_TABLE = build_feeds()


def load_kernel(mine, out, sems):
    def copy(i):
        return pltpu.make_async_copy(mine.at[i], out.at[i], sems.at[i])

    def start(i, carry):
        copy(i).start()
        return carry

    def wait(i, carry):
        copy(i).wait()
        return carry

    lax.fori_loop(0, out.shape[0], start, 0)
    lax.fori_loop(0, out.shape[0], wait, 0)


def load_core(mine):
    return pl.pallas_call(
        load_kernel, in_specs=[ANY], out_specs=pl.BlockSpec(memory_space=pltpu.VMEM),
        out_shape=jax.ShapeDtypeStruct(mine.shape, BF),
        scratch_shapes=[pltpu.SemaphoreType.DMA((mine.shape[0],))],
        cost_estimate=pl.CostEstimate(flops=0, bytes_accessed=4 * mine.size, transcendentals=0),
        compiler_params=pltpu.CompilerParams(vmem_limit_bytes=12 << 20),
        name="load_core",
    )(mine)


def both_kernel(mine, pair, out, room, sems):
    def copy(i):
        return pltpu.make_async_copy(pair.at[i], room.at[i], sems.at[i])

    def start(i, carry):
        copy(i).start()
        return carry

    def add(i, carry):
        copy(i).wait()
        out[i] = mine[i] + room[i]
        return carry

    lax.fori_loop(0, out.shape[0], start, 0)
    lax.fori_loop(0, out.shape[0], add, 0)


def add_cores(mine, pair):
    whole = pl.BlockSpec(memory_space=pltpu.VMEM)
    return pl.pallas_call(
        both_kernel, in_specs=[whole, ANY], out_specs=whole,
        out_shape=jax.ShapeDtypeStruct(mine.shape, BF),
        scratch_shapes=[pltpu.VMEM(mine.shape, BF), pltpu.SemaphoreType.DMA((mine.shape[0],))],
        input_output_aliases={0: 0},
        cost_estimate=pl.CostEstimate(flops=0, bytes_accessed=6 * mine.size, transcendentals=0),
        compiler_params=pltpu.CompilerParams(vmem_limit_bytes=20 << 20),
        name="add_cores",
    )(mine, pair)


def add_kernel(flags, row, feed, own, *refs):
    out, acc = refs[-2], refs[-1]

    def slot(r, carry):
        acc[...] = own[0, r].astype(F32)
        for ref, column in zip(refs[:-2], flags):
            @pl.when(feed[column] == 1)
            def _():
                acc[...] += ref[r].astype(F32)
        out[r] = acc[...].astype(out.dtype)
        return carry

    lax.fori_loop(0, out.shape[0], slot, 0)


def add_block(row, feed, block_column, sums, arrays, flags, dtype):
    slots = sums.shape[1]
    shape = sums.shape[1:]
    pieces = 2 if slots % 2 == 0 else 1
    piece = (slots // pieces,) + shape[1:]
    by_block = pl.BlockSpec((1,) + piece, lambda i, rw, fd: (rw[block_column], i, 0, 0))
    plain = pl.BlockSpec(piece, lambda i, rw, fd: (i, 0, 0))
    return pl.pallas_call(
        partial(add_kernel, tuple(flags)),
        grid_spec=pltpu.PrefetchScalarGridSpec(
            num_scalar_prefetch=2, grid=(pieces,),
            in_specs=[by_block] + [plain] * len(arrays), out_specs=plain,
            scratch_shapes=[pltpu.VMEM(piece[1:], F32)]),
        out_shape=jax.ShapeDtypeStruct(shape, dtype),
        cost_estimate=pl.CostEstimate(
            flops=0, bytes_accessed=2 * sums[0].size * (2 + len(arrays)), transcendentals=0),
        compiler_params=pltpu.CompilerParams(vmem_limit_bytes=12 << 20),
        name="add_block",
    )(row, feed, sums, *arrays)


def partners():
    size = lax.axis_size("batch")
    steps, bit = [], 1
    while bit < size:
        steps.append(("batch", tuple((i, i ^ bit) for i in range(size))))
        bit *= 2
    return steps + [("seq", SWAP)]


def reduce_slots(mine, theirs, small):
    me = lax.axis_index("batch")
    takes = jnp.asarray(TABLE)[me][0::3]
    row = jnp.concatenate([jnp.where(takes == DUMMY, 0, takes), jnp.stack([me])])
    feed = jnp.asarray(FEED_TABLE)[me]
    pair = lax.ppermute(theirs, "seq", SWAP)
    mine = mine.reshape((16, -1) + mine.shape[1:])
    sums = add_cores(load_core(mine), pair.reshape(mine.shape))
    steps = partners()
    early = small
    for step in (steps.pop(-2), steps.pop(-2)):
        early = early + lax.ppermute(early, *step)
    small = early
    before = []
    arrived, ready = {}, lax.optimization_barrier((row, early))[0]
    for turn in reversed(range(RING_ROUNDS)):
        gives = []
        now = [i for i, move in enumerate(MOVES) if move[0] == turn]
        for i in now:
            give = add_block(ready, feed, i, sums, [arrived[m] for m, _ in FEEDS[i]],
                             [column for _, column in FEEDS[i]], BF)
            gives.append(give)
            back = tuple((target, source) for source, target in MOVES[i][2])
            arrived[i] = lax.ppermute(give, "batch", back)
        late = [arrived[i] for i in before]
        ready, small, *late = lax.optimization_barrier((row, small, *late, *gives))
        arrived.update(zip(before, late))
        before = now
        if steps:
            small = small + lax.ppermute(small, *steps.pop(0))
    for step in steps:
        small = small + lax.ppermute(small, *step)
    last = FEEDS[len(MOVES)]
    total = add_block(row, feed, len(MOVES), sums, [arrived[m] for m, _ in last],
                      [column for _, column in last], F32)
    return total, small


def slot_table(owners, capacity):
    panel_index = jnp.arange(owners.shape[0], dtype=jnp.int32)
    same_owner = (owners[:, None] == owners[None, :]) & (
        panel_index[None, :] < panel_index[:, None]
    )
    rank_within = jnp.sum(same_owner.astype(jnp.int32), axis=1)
    return owners * capacity + rank_within


def adam_update(weight, first_old, second_old, grad_now, step_count):
    step_float = step_count[0].astype(jnp.float32)
    first_new = beta_first * first_old + (1.0 - beta_first) * grad_now
    second_new = beta_second * second_old + (1.0 - beta_second) * grad_now * grad_now
    first_hat = first_new / (1.0 - jnp.power(beta_first, step_float))
    second_hat = second_new / (1.0 - jnp.power(beta_second, step_float))
    weight_new = weight - learn_rate * (
        first_hat / (jnp.sqrt(second_hat) + adam_eps) + decay_rate * weight
    )
    return (weight_new, first_new, second_new)


def local(
    tokens,
    grad_out,
    lengths,
    owners,
    weight_slots,
    first_slots,
    second_slots,
    small_params,
    small_first,
    small_second,
    step_count,
):
    capacity = weight_slots.shape[0]
    block_rows, features = tokens.shape[1:]
    slot_of = slot_table(owners, capacity)
    devices = lax.axis_size("seq") * lax.axis_size("batch")
    device = lax.axis_index("seq") * lax.axis_size("batch") + lax.axis_index("batch")
    limits = lengths - lax.axis_index("seq") * block_rows
    core = lax.axis_index("seq")
    batch = lax.axis_size("batch")
    half = batch * capacity
    owner_core = (owners >= batch).astype(jnp.int32)
    back = slot_of - owner_core * half + jnp.where(owner_core == core, 0, half)
    gathered = lax.all_gather(weight_slots.astype(BF), ("seq", "batch"), axis=0, tiled=True)
    q, k, v, ctx, probs, mixed, zh, rstd = attn_fwd(tokens, gathered, small_params, limits, slot_of)
    bias_hidden = small_params[8:].reshape(1, -1)
    layer_out, d_mixed, sums_ffn, d_bias, mine, theirs = ffn(
        mixed.reshape(-1, features), grad_out.reshape(-1, features), gathered, small_params,
        bias_hidden, slot_of, back, half)
    grad_in, sums_attn, mine, theirs = attn_bwd(
        d_mixed.reshape(tokens.shape), zh, rstd, tokens, q, k, v, ctx, probs, gathered,
        small_params, limits, slot_of, back, mine, theirs)
    small_local = jnp.concatenate(
        [sums_attn[0:2], sums_ffn[0:2], sums_attn[2:5], sums_ffn[2:3],
         d_bias.reshape(-1, features)], axis=0)
    if batch == 16 and lax.axis_size("seq") == 2:
        grad_slots, small_grad = reduce_slots(mine, theirs, small_local)
    else:
        both = jnp.where(core == 0, jnp.stack([mine, theirs]), jnp.stack([theirs, mine]))
        grad_slots = lax.psum_scatter(
            both.reshape((-1,) + mine.shape[1:]), ("seq", "batch"), scatter_dimension=0,
            tiled=True).astype(jnp.float32)
        small_grad = small_local
        for step in partners():
            small_grad = small_grad + lax.ppermute(small_grad, *step)
    held = jnp.sum((owners == device).astype(jnp.int32))
    used = jnp.arange(capacity, dtype=jnp.int32) < held
    grad_slots = jnp.where(used[:, None, None], grad_slots, 0.0)
    new_slots, new_first_slots, new_second_slots = adam_update(
        weight_slots, first_slots, second_slots, grad_slots, step_count
    )
    new_small, new_small_first, new_small_second = adam_update(
        small_params, small_first, small_second, small_grad, step_count
    )
    return (
        layer_out.reshape(tokens.shape),
        grad_in,
        grad_slots,
        new_slots,
        new_first_slots,
        new_second_slots,
        small_grad,
        new_small,
        new_small_first,
        new_small_second,
    )


def solution(mesh):
    in_specs = (
        P("batch", "seq", None),
        P("batch", "seq", None),
        P("batch"),
        P(),
        P(("seq", "batch"), None, None),
        P(("seq", "batch"), None, None),
        P(("seq", "batch"), None, None),
        P(),
        P(),
        P(),
        P(),
    )
    out_specs = (
        P("batch", "seq", None),
        P("batch", "seq", None),
        P(("seq", "batch"), None, None),
        P(("seq", "batch"), None, None),
        P(("seq", "batch"), None, None),
        P(("seq", "batch"), None, None),
        P(),
        P(),
        P(),
        P(),
    )
    return jax.shard_map(local, mesh=mesh, in_specs=in_specs, out_specs=out_specs, check_vma=False)
```

```python
from functools import partial
import math

import jax
import jax.numpy as jnp
import numpy as np
from jax import lax
from jax.experimental import pallas as pl
from jax.experimental.pallas import tpu as pltpu
from jax.sharding import PartitionSpec as P

beta_first = 0.9
beta_second = 0.999
adam_eps = 1e-08
learn_rate = 0.2
decay_rate = 0.01
SWAP = ((0, 1), (1, 0))

HEAD_DIM = 64
PANEL = 32
norm_eps = 1e-06
masked_score = -30.0
LANES = 128
BF = jnp.bfloat16
F32 = jnp.float32
ANY = pl.BlockSpec(memory_space=pl.ANY)


def mm(a, b):
    return lax.dot_general(a, b, (((1,), (0,)), ((), ())), preferred_element_type=F32)


def mm_nt(a, b):
    return lax.dot_general(a, b, (((1,), (1,)), ((), ())), preferred_element_type=F32)


def mm_tn(a, b):
    return lax.dot_general(a, b, (((0,), (0,)), ((), ())), preferred_element_type=F32)


def normalize(z):
    centre = z - jnp.mean(z, axis=-1, keepdims=True)
    rstd = lax.rsqrt(jnp.mean(centre * centre, axis=-1, keepdims=True) + norm_eps)
    return centre * rstd, rstd


def norm_back(zh, rstd, t):
    mean_t = jnp.mean(t, axis=-1, keepdims=True)
    mean_tz = jnp.mean(t * zh, axis=-1, keepdims=True)
    return (t - mean_t - zh * mean_tz) * rstd


def lane_half(shape, half):
    lane = lax.broadcasted_iota(jnp.int32, shape, len(shape) - 1)
    return (lane < HEAD_DIM) if half == 0 else (lane >= HEAD_DIM)


def rows_of(panels, start, count):
    return panels[start // PANEL:(start + count) // PANEL].reshape(count, panels.shape[-1])


def fetch_panels(slots, first, target, place, sem):
    def one(i, carry):
        pltpu.make_async_copy(slots.at[place[first + i]], target.at[i], sem).start()
        return carry
    lax.fori_loop(0, target.shape[0], one, 0)


def fetch_wait(slots, target, sem):
    pltpu.make_async_copy(slots.at[pl.ds(0, target.shape[0])], target, sem).wait()


def send_panels(stage, first, mine, theirs, back, sem):
    half = mine.shape[0]

    def one(i, carry):
        slot = back[first + i]

        @pl.when(slot < half)
        def _():
            pltpu.make_async_copy(stage.at[i], mine.at[slot], sem).start()

        @pl.when(slot >= half)
        def _():
            pltpu.make_async_copy(stage.at[i], theirs.at[slot - half], sem).start()

        return carry

    lax.fori_loop(0, stage.shape[0], one, 0)


def send_wait(stage, mine, sem):
    pltpu.make_async_copy(stage, mine.at[pl.ds(0, stage.shape[0])], sem).wait()


def attn_fwd_kernel(limits, place, x_ref, slots_ref, small_ref, q_ref, k_ref, v_ref, c_ref, p_ref,
                    mixed_ref, zh_ref, rstd_ref, w_ref, w_sem):
    step = pl.program_id(0)
    groups = x_ref.shape[-1] // LANES // PAIRS_FWD
    seq, group = step // groups, step % groups
    d = x_ref.shape[-1]
    block = x_ref.shape[1]

    @pl.when(step == 0)
    def _():
        fetch_panels(slots_ref, 0, w_ref, place, w_sem)
        fetch_wait(slots_ref, w_ref, w_sem)

    @pl.when(group == 0)
    def _():
        x = x_ref[0]
        q = mm(x, rows_of(w_ref, 0, d)) + small_ref[4:5, :]
        q_ref[0] = (q.astype(BF).astype(F32) * 0.125).astype(BF)
        k_ref[0] = mm(x, rows_of(w_ref, d, d)).astype(BF)
        v_ref[0] = (mm(x, rows_of(w_ref, 2 * d, d)) + small_ref[5:6, :]).astype(BF)

    limit = limits[seq]
    key = lax.broadcasted_iota(jnp.int32, (block, block), 0)
    for n in range(PAIRS_FWD):
        lanes = pl.ds(pl.multiple_of((group * PAIRS_FWD + n) * LANES, LANES), LANES)
        qp, kp, vp = q_ref[0, :, lanes], k_ref[0, :, lanes], v_ref[0, :, lanes]
        vt = vp.T
        parts = []
        for half in range(2):
            km = jnp.where(lane_half(kp.shape, half), kp, jnp.zeros_like(kp))
            s = mm_nt(km, qp)
            s = jnp.where(key < limit, s, masked_score)
            top = jnp.max(s, axis=0, keepdims=True)
            e = jnp.exp(s - top)
            total = jnp.sum(e, axis=0, keepdims=True)
            p = (e * (1.0 / total)).astype(BF)
            p_ref[2 * n + half] = p
            parts.append(mm(vt[half * HEAD_DIM:(half + 1) * HEAD_DIM], p))
        ctx_t = jnp.concatenate(parts, axis=0)
        c_ref[0, :, lanes] = ctx_t.T.astype(BF)

    @pl.when(group == groups - 1)
    def _():
        u = x_ref[0].astype(F32) + mm(c_ref[0], rows_of(w_ref, 3 * d, d)) + small_ref[6:7, :]
        zh, rstd = normalize(u)
        zh_ref[0] = zh
        rstd_ref[0] = rstd
        mixed_ref[0] = (zh * small_ref[0:1, :] + small_ref[1:2, :]).astype(BF)


def attn_fwd(x, gathered, small, limits, place):
    seqs, block, d = x.shape
    pairs = d // LANES
    groups = pairs // PAIRS_FWD
    by_seq = lambda shape: pl.BlockSpec((1,) + shape, lambda i, lim, pr: (i // groups, 0, 0))
    whole = lambda a: pl.BlockSpec(a, lambda i, lim, pr: (0, 0), pipeline_mode=pl.Buffered(1))
    act = jax.ShapeDtypeStruct((seqs, block, d), BF)
    return pl.pallas_call(
        attn_fwd_kernel,
        grid_spec=pltpu.PrefetchScalarGridSpec(
            num_scalar_prefetch=2,
            grid=(seqs * groups,),
            in_specs=[by_seq((block, d)), ANY, whole(small.shape)],
            out_specs=[by_seq((block, d))] * 4
            + [pl.BlockSpec((2 * PAIRS_FWD, block, block), lambda i, lim, pr: (i, 0, 0))]
            + [by_seq((block, d)), by_seq((block, d)), by_seq((block, 1))],
            scratch_shapes=[pltpu.VMEM((4 * d // PANEL, PANEL, d), BF), pltpu.SemaphoreType.DMA],
        ),
        out_shape=[act, act, act, act,
                   jax.ShapeDtypeStruct((seqs * 2 * pairs, block, block), BF),
                   act,
                   jax.ShapeDtypeStruct((seqs, block, d), F32),
                   jax.ShapeDtypeStruct((seqs, block, 1), F32)],
        compiler_params=pltpu.CompilerParams(vmem_limit_bytes=56 << 20, dimension_semantics=("arbitrary",)),
        name="attn_fwd",
    )(limits, place, x, gathered, small)


ROWS = 512
PAIRS_FWD = 2
PAIRS_BWD = 2
CHUNK = 1024


def ffn_kernel(place, back, mixed_ref, go_ref, w_hbm, small_ref, bh_ref,
               out_ref, dmixed_ref, sums_ref, dbh_ref, mine, theirs,
               w1, w2, hid, gp, acc, df, dyb, stage, w_sem, s_sem):
    d = mixed_ref.shape[-1]
    tokens = mixed_ref.shape[0]
    ff = bh_ref.shape[1]
    chunks = ff // CHUNK
    tiles = tokens // ROWS
    panels = CHUNK // PANEL
    first1 = 4 * d // PANEL
    first2 = first1 + ff // PANEL

    def start(c, carry):
        fetch_panels(w_hbm, first1 + c * panels, w1.at[c], place, w_sem.at[0, c])
        fetch_panels(w_hbm, first2 + c * panels, w2.at[c], place, w_sem.at[1, c])
        return carry

    lax.fori_loop(0, chunks, start, 0)

    def up(c, carry):
        fetch_wait(w_hbm, w1.at[c], w_sem.at[0, c])
        fetch_wait(w_hbm, w2.at[c], w_sem.at[1, c])
        cols = pl.ds(pl.multiple_of(c * CHUNK, CHUNK), CHUNK)
        w1c, w2c = w1[c].reshape(CHUNK, d), w2[c].reshape(CHUNK, d)
        bias = bh_ref[0:1, cols]
        for r in range(tiles):
            rows = pl.ds(r * ROWS, ROWS)
            f = mm_nt(mixed_ref[rows, :], w1c) + bias
            half_erf = 0.5 * lax.erf(f * (1.0 / math.sqrt(2.0))) + 0.5
            h = (f * half_erf).astype(BF)
            hid[rows, cols] = h
            gp[rows, cols] = (half_erf + f * (jnp.exp(-0.5 * f * f) * (1.0 / math.sqrt(2.0 * math.pi)))).astype(BF)
            part = mm(h, w2c)
            acc[rows, :] = jnp.where(c == 0, part, acc[rows, :] + part)
        return carry

    lax.fori_loop(0, chunks, up, 0)

    sums_ref[...] = jnp.zeros_like(sums_ref)

    def middle(r, carry):
        rows = pl.ds(pl.multiple_of(r * ROWS, ROWS), ROWS)
        rr = mixed_ref[rows, :].astype(F32) + acc[rows, :] + small_ref[7:8, :]
        zh, rstd = normalize(rr)
        out_ref[rows, :] = (zh * small_ref[2:3, :] + small_ref[3:4, :]).astype(BF)
        e = go_ref[rows, :].astype(F32)
        dr = norm_back(zh, rstd, e * small_ref[2:3, :])
        dy = dr.astype(BF)
        dyb[rows, :] = dy
        acc[rows, :] = dr
        sums_ref[0:1, :] += jnp.sum(e * zh, axis=0, keepdims=True)
        sums_ref[1:2, :] += jnp.sum(e, axis=0, keepdims=True)
        sums_ref[2:3, :] += jnp.sum(dy.astype(F32), axis=0, keepdims=True)
        return carry

    lax.fori_loop(0, tiles, middle, 0)

    def down(c, carry):
        cols = pl.ds(pl.multiple_of(c * CHUNK, CHUNK), CHUNK)
        w1c, w2c = w1[c].reshape(CHUNK, d), w2[c].reshape(CHUNK, d)
        dbh = jnp.zeros((1, CHUNK), F32)
        for r in range(tiles):
            rows = pl.ds(r * ROWS, ROWS)
            dfr = (mm_nt(dyb[rows, :], w2c) * gp[rows, cols].astype(F32)).astype(BF)
            df[rows, :] = dfr
            dbh += jnp.sum(dfr.astype(F32), axis=0, keepdims=True)
            acc[rows, :] += mm(dfr, w1c)
        dbh_ref[0:1, cols] = dbh

        @pl.when(c > 0)
        def _():
            send_wait(stage.at[0], mine, s_sem.at[0])
            send_wait(stage.at[1], mine, s_sem.at[1])

        stage[0] = mm_tn(df[...], mixed_ref[...]).astype(BF).reshape(panels, PANEL, d)
        send_panels(stage.at[0], first1 + c * panels, mine, theirs, back, s_sem.at[0])
        stage[1] = mm_tn(hid[:, cols], dyb[...]).astype(BF).reshape(panels, PANEL, d)
        send_panels(stage.at[1], first2 + c * panels, mine, theirs, back, s_sem.at[1])
        return carry

    lax.fori_loop(0, chunks, down, 0)
    dmixed_ref[...] = acc[...].astype(BF)
    send_wait(stage.at[0], mine, s_sem.at[0])
    send_wait(stage.at[1], mine, s_sem.at[1])


def ffn(mixed, go, gathered, small, bh, place, back, half):
    tokens, d = mixed.shape
    ff = bh.shape[1]
    full = lambda shape: pl.BlockSpec(shape, lambda i, pr, bk: (0,) * len(shape))
    return pl.pallas_call(
        ffn_kernel,
        grid_spec=pltpu.PrefetchScalarGridSpec(
            num_scalar_prefetch=2,
            grid=(1,),
            in_specs=[full((tokens, d)), full((tokens, d)), ANY,
                      full(small.shape), full(bh.shape)],
            out_specs=[full((tokens, d)), full((tokens, d)), full((8, d)), full((1, ff)),
                       ANY, ANY],
            scratch_shapes=[
                pltpu.VMEM((ff // CHUNK, CHUNK // PANEL, PANEL, d), BF),
                pltpu.VMEM((ff // CHUNK, CHUNK // PANEL, PANEL, d), BF),
                pltpu.VMEM((tokens, ff), BF), pltpu.VMEM((tokens, ff), BF),
                pltpu.VMEM((tokens, d), F32), pltpu.VMEM((tokens, CHUNK), BF),
                pltpu.VMEM((tokens, d), BF), pltpu.VMEM((2, CHUNK // PANEL, PANEL, d), BF),
                pltpu.SemaphoreType.DMA((2, ff // CHUNK)), pltpu.SemaphoreType.DMA((2,)),
            ],
        ),
        out_shape=[jax.ShapeDtypeStruct((tokens, d), BF), jax.ShapeDtypeStruct((tokens, d), BF),
                   jax.ShapeDtypeStruct((8, d), F32), jax.ShapeDtypeStruct((1, ff), F32),
                   jax.ShapeDtypeStruct((half, PANEL, d), BF), jax.ShapeDtypeStruct((half, PANEL, d), BF)],
        compiler_params=pltpu.CompilerParams(vmem_limit_bytes=60 << 20, dimension_semantics=("arbitrary",)),
        name="ffn",
    )(place, back, mixed, go, gathered, small, bh)


def attn_bwd_kernel(limits, place, back, dmixed_ref, zh_ref, rstd_ref, x_ref, q_ref, k_ref, v_ref,
                    c_ref, p_ref, w_hbm, small_ref, mine_in, theirs_in,
                    gin_ref, sums_ref, mine, theirs,
                    dctx, dq, dk, dv, dw, stage, w_ref, s_sem, w_sem):
    step = pl.program_id(0)
    groups = x_ref.shape[-1] // LANES // PAIRS_BWD
    seq, group = step // groups, step % groups
    d = x_ref.shape[-1]
    block = x_ref.shape[1]
    tiles = block // ROWS

    @pl.when(step == 0)
    def _():
        fetch_panels(w_hbm, 0, w_ref, place, w_sem)
        dw[...] = jnp.zeros_like(dw)
        sums_ref[...] = jnp.zeros_like(sums_ref)
        fetch_wait(w_hbm, w_ref, w_sem)

    @pl.when(group == 0)
    def _():
        for r in range(tiles):
            rows = pl.ds(r * ROWS, ROWS)
            e = dmixed_ref[0, rows, :].astype(F32)
            zh = zh_ref[0, rows, :]
            du = norm_back(zh, rstd_ref[0, rows, :], e * small_ref[0:1, :])
            da = du.astype(BF)
            gin_ref[0, rows, :] = du
            sums_ref[0:1, :] += jnp.sum(e * zh, axis=0, keepdims=True)
            sums_ref[1:2, :] += jnp.sum(e, axis=0, keepdims=True)
            sums_ref[4:5, :] += jnp.sum(da.astype(F32), axis=0, keepdims=True)
            dctx[rows, :] = mm_nt(da, rows_of(w_ref, 3 * d, d)).astype(BF)
            dw[pl.ds(3 * d, d), :] += mm_tn(c_ref[0, rows, :], da)

    limit = limits[seq]
    key = lax.broadcasted_iota(jnp.int32, (block, block), 0)
    for n in range(PAIRS_BWD):
        lanes = pl.ds(pl.multiple_of((group * PAIRS_BWD + n) * LANES, LANES), LANES)
        qp, kp, vp, dcp = q_ref[0, :, lanes], k_ref[0, :, lanes], v_ref[0, :, lanes], dctx[:, lanes]
        kt = kp.T
        prod_t = (dcp.astype(F32) * c_ref[0, :, lanes].astype(F32)).T
        dqt, dks, dvs = [], [], []
        for half in range(2):
            vm = jnp.where(lane_half(vp.shape, half), vp, jnp.zeros_like(vp))
            dp = mm_nt(vm, dcp)
            delta = jnp.sum(prod_t[half * HEAD_DIM:(half + 1) * HEAD_DIM], axis=0, keepdims=True)
            p = p_ref[2 * n + half]
            ds = jnp.where(key < limit, p.astype(F32) * (dp - delta), 0.0).astype(BF)
            dqt.append(mm(kt[half * HEAD_DIM:(half + 1) * HEAD_DIM], ds))
            dks.append(mm(ds, qp))
            dvs.append(mm(p, dcp))
        low = lane_half(qp.shape, 0)
        dq[:, lanes] = (jnp.concatenate(dqt, axis=0) * 0.125).T.astype(BF)
        dk[:, lanes] = jnp.where(low, dks[0], dks[1]).astype(BF)
        dv[:, lanes] = jnp.where(low, dvs[0], dvs[1]).astype(BF)

    @pl.when(group == groups - 1)
    def _():
        x = x_ref[0]
        gin_ref[0] += (mm_nt(dq[...], rows_of(w_ref, 0, d)) + mm_nt(dk[...], rows_of(w_ref, d, d))
                       + mm_nt(dv[...], rows_of(w_ref, 2 * d, d)))
        dw[pl.ds(0, d), :] += mm_tn(x, dq[...])
        dw[pl.ds(d, d), :] += mm_tn(x, dk[...])
        dw[pl.ds(2 * d, d), :] += mm_tn(x, dv[...])
        sums_ref[2:3, :] += jnp.sum(dq[...].astype(F32), axis=0, keepdims=True)
        sums_ref[3:4, :] += jnp.sum(dv[...].astype(F32), axis=0, keepdims=True)

    @pl.when(step == pl.num_programs(0) - 1)
    def _():
        stage[...] = dw[...].astype(BF).reshape(stage.shape)
        send_panels(stage, 0, mine, theirs, back, s_sem)
        send_wait(stage, mine, s_sem)


def attn_bwd(dmixed, zh, rstd, x, q, k, v, c, p, gathered, small, limits, place, back, mine, theirs):
    seqs, block, d = x.shape
    pairs = d // LANES
    groups = pairs // PAIRS_BWD
    by_seq = lambda shape: pl.BlockSpec((1,) + shape, lambda i, lim, pr, bk: (i // groups, 0, 0))
    whole = lambda a: pl.BlockSpec(a, lambda i, lim, pr, bk: (0, 0), pipeline_mode=pl.Buffered(1))
    return pl.pallas_call(
        attn_bwd_kernel,
        grid_spec=pltpu.PrefetchScalarGridSpec(
            num_scalar_prefetch=3,
            grid=(seqs * groups,),
            in_specs=[by_seq((block, d)), by_seq((block, d)), by_seq((block, 1))]
            + [by_seq((block, d))] * 5
            + [pl.BlockSpec((2 * PAIRS_BWD, block, block), lambda i, lim, pr, bk: (i, 0, 0)),
               ANY, whole(small.shape), ANY, ANY],
            out_specs=[by_seq((block, d)), pl.BlockSpec((8, d), lambda i, lim, pr, bk: (0, 0)),
                       ANY, ANY],
            scratch_shapes=[pltpu.VMEM((block, d), BF)] * 4
            + [pltpu.VMEM((4 * d, d), F32), pltpu.VMEM((4 * d // PANEL, PANEL, d), BF),
               pltpu.VMEM((4 * d // PANEL, PANEL, d), BF), pltpu.SemaphoreType.DMA, pltpu.SemaphoreType.DMA],
        ),
        out_shape=[jax.ShapeDtypeStruct((seqs, block, d), F32), jax.ShapeDtypeStruct((8, d), F32),
                   jax.ShapeDtypeStruct(mine.shape, BF), jax.ShapeDtypeStruct(mine.shape, BF)],
        input_output_aliases={14: 2, 15: 3},
        compiler_params=pltpu.CompilerParams(vmem_limit_bytes=60 << 20, dimension_semantics=("arbitrary",)),
        name="attn_bwd",
    )(limits, place, back, dmixed, zh, rstd, x, q, k, v, c, p, gathered, small, mine, theirs)


RING_ROUNDS = 5
LINKS = ("x", "y", "u", "d")
NEW_BLOCK = {
    (0, 0, "x"): (1, 0, 0), (0, 0, "y"): (0, 1, 0), (0, 0, "d"): (0, 0, 1),
    (0, 1, "x"): (1, 0, 1), (0, 1, "y"): (1, 1, 0), (0, 1, "d"): (0, 0, 2),
    (0, 2, "x"): (1, 0, 2), (0, 2, "y"): (0, 1, 2), (0, 2, "d"): (0, 0, 3),
    (0, 3, "x"): (1, 0, 3), (0, 3, "y"): (0, 1, 3), (0, 3, "d"): (1, 1, 2),
    (0, 4, "x"): (1, 1, 3), (0, 4, "y"): (1, 1, 1), (0, 4, "d"): (0, 1, 1),
    (1, 0, "x"): (1, 0, 1), (1, 0, "y"): (0, 1, 1), (1, 0, "u"): (0, 0, 0), (1, 0, "d"): (0, 0, 2),
    (1, 1, "x"): (1, 0, 2), (1, 1, "y"): (0, 1, 2), (1, 1, "u"): (1, 0, 0), (1, 1, "d"): (0, 0, 3),
    (1, 2, "x"): (1, 1, 2), (1, 2, "y"): (0, 1, 3), (1, 2, "u"): (0, 1, 0), (1, 2, "d"): (1, 0, 3),
    (1, 3, "x"): (1, 1, 0), (1, 3, "y"): (1, 1, 3), (1, 3, "d"): (1, 1, 1),
}
DUMMY = 16


def neighbour(chip, link):
    if link == "x":
        return chip ^ 1
    if link == "y":
        return chip ^ 2
    if link == "u":
        return chip - 4 if chip >= 4 else None
    return chip + 4 if chip < 12 else None


def received_block(chip, turn, link):
    layer = chip >> 2
    if layer < 2:
        block = NEW_BLOCK.get((layer, turn, link))
        if block is None:
            return None
        return block[2] * 4 + ((chip & 3) ^ (block[1] * 2 + block[0]))
    block = NEW_BLOCK.get((3 - layer, turn, {"u": "d", "d": "u"}.get(link, link)))
    if block is None:
        return None
    return (3 - block[2]) * 4 + ((chip & 3) ^ (block[1] * 2 + block[0]))


def build_schedule():
    moves, columns = [], []
    held = [{chip: -1} for chip in range(16)]
    for turn in range(RING_ROUNDS):
        fresh = []
        for link in LINKS:
            pairs, takes, gives, given = [], [DUMMY] * 16, [DUMMY] * 16, {}
            for chip in range(16):
                block = received_block(chip, turn, link)
                if block is None:
                    continue
                source = neighbour(chip, link)
                pairs.append((source, chip))
                takes[chip] = block
                gives[source] = block
                given[source] = held[source][block]
                fresh.append((chip, block, len(moves)))
            if not pairs:
                continue
            sources = sorted(set(given.values()))
            which = [sources.index(given.get(chip, sources[0])) for chip in range(16)]
            moves.append((turn, link, tuple(pairs), tuple(sources)))
            columns += [takes, which, gives]
        for chip, block, move in fresh:
            held[chip][block] = move
    return moves, np.array(columns, np.int32).T


MOVES, TABLE = build_schedule()


def feeders(move):
    takes = [received_block(chip, MOVES[move][0], MOVES[move][1]) for chip in range(16)]
    return feeding(takes, MOVES[move][0])


def feeding(blocks, turn):
    found = []
    for later, (after, link, pairs, _) in enumerate(MOVES):
        if after <= turn:
            continue
        chips = [
            source for source, target in pairs
            if blocks[source] is not None and received_block(target, after, link) == blocks[source]
        ]
        if chips:
            found.append((later, tuple(chips)))
    return found


def build_feeds():
    feeds, columns = [], []
    for move in range(len(MOVES) + 1):
        found = feeders(move) if move < len(MOVES) else feeding(list(range(16)), -1)
        feeds.append([(later, len(columns) + i) for i, (later, _) in enumerate(found)])
        columns += [[int(chip in chips) for chip in range(16)] for _, chips in found]
    return feeds, np.array(columns, np.int32).T


FEEDS, FEED_TABLE = build_feeds()


def load_kernel(mine, out, sems):
    def copy(i):
        return pltpu.make_async_copy(mine.at[i], out.at[i], sems.at[i])

    def start(i, carry):
        copy(i).start()
        return carry

    def wait(i, carry):
        copy(i).wait()
        return carry

    lax.fori_loop(0, out.shape[0], start, 0)
    lax.fori_loop(0, out.shape[0], wait, 0)


def load_core(mine):
    return pl.pallas_call(
        load_kernel, in_specs=[ANY], out_specs=pl.BlockSpec(memory_space=pltpu.VMEM),
        out_shape=jax.ShapeDtypeStruct(mine.shape, BF),
        scratch_shapes=[pltpu.SemaphoreType.DMA((mine.shape[0],))],
        cost_estimate=pl.CostEstimate(flops=0, bytes_accessed=4 * mine.size, transcendentals=0),
        compiler_params=pltpu.CompilerParams(vmem_limit_bytes=12 << 20),
        name="load_core",
    )(mine)


def both_kernel(mine, pair, out, room, sems):
    def copy(i):
        return pltpu.make_async_copy(pair.at[i], room.at[i], sems.at[i])

    def start(i, carry):
        copy(i).start()
        return carry

    def add(i, carry):
        copy(i).wait()
        out[i] = mine[i] + room[i]
        return carry

    lax.fori_loop(0, out.shape[0], start, 0)
    lax.fori_loop(0, out.shape[0], add, 0)


def add_cores(mine, pair):
    whole = pl.BlockSpec(memory_space=pltpu.VMEM)
    return pl.pallas_call(
        both_kernel, in_specs=[whole, ANY], out_specs=whole,
        out_shape=jax.ShapeDtypeStruct(mine.shape, BF),
        scratch_shapes=[pltpu.VMEM(mine.shape, BF), pltpu.SemaphoreType.DMA((mine.shape[0],))],
        input_output_aliases={0: 0},
        cost_estimate=pl.CostEstimate(flops=0, bytes_accessed=6 * mine.size, transcendentals=0),
        compiler_params=pltpu.CompilerParams(vmem_limit_bytes=20 << 20),
        name="add_cores",
    )(mine, pair)


def add_kernel(flags, row, feed, own, *refs):
    out, acc = refs[-2], refs[-1]

    def slot(r, carry):
        acc[...] = own[0, r].astype(F32)
        for ref, column in zip(refs[:-2], flags):
            @pl.when(feed[column] == 1)
            def _():
                acc[...] += ref[r].astype(F32)
        out[r] = acc[...].astype(out.dtype)
        return carry

    lax.fori_loop(0, out.shape[0], slot, 0)


def add_block(row, feed, block_column, sums, arrays, flags, dtype):
    slots = sums.shape[1]
    shape = sums.shape[1:]
    pieces = 2 if slots % 2 == 0 else 1
    piece = (slots // pieces,) + shape[1:]
    by_block = pl.BlockSpec((1,) + piece, lambda i, rw, fd: (rw[block_column], i, 0, 0))
    plain = pl.BlockSpec(piece, lambda i, rw, fd: (i, 0, 0))
    return pl.pallas_call(
        partial(add_kernel, tuple(flags)),
        grid_spec=pltpu.PrefetchScalarGridSpec(
            num_scalar_prefetch=2, grid=(pieces,),
            in_specs=[by_block] + [plain] * len(arrays), out_specs=plain,
            scratch_shapes=[pltpu.VMEM(piece[1:], F32)]),
        out_shape=jax.ShapeDtypeStruct(shape, dtype),
        cost_estimate=pl.CostEstimate(
            flops=0, bytes_accessed=2 * sums[0].size * (2 + len(arrays)), transcendentals=0),
        compiler_params=pltpu.CompilerParams(vmem_limit_bytes=12 << 20),
        name="add_block",
    )(row, feed, sums, *arrays)


def partners():
    size = lax.axis_size("batch")
    steps, bit = [], 1
    while bit < size:
        steps.append(("batch", tuple((i, i ^ bit) for i in range(size))))
        bit *= 2
    return steps + [("seq", SWAP)]


def reduce_slots(mine, theirs, small):
    me = lax.axis_index("batch")
    takes = jnp.asarray(TABLE)[me][0::3]
    row = jnp.concatenate([jnp.where(takes == DUMMY, 0, takes), jnp.stack([me])])
    feed = jnp.asarray(FEED_TABLE)[me]
    pair = lax.ppermute(theirs, "seq", SWAP)
    mine = mine.reshape((16, -1) + mine.shape[1:])
    sums = add_cores(load_core(mine), pair.reshape(mine.shape))
    steps = partners()
    early = small
    for step in (steps.pop(-2), steps.pop(-2)):
        early = early + lax.ppermute(early, *step)
    small = early
    before = []
    arrived, ready = {}, lax.optimization_barrier((row, early))[0]
    for turn in reversed(range(RING_ROUNDS)):
        gives = []
        now = [i for i, move in enumerate(MOVES) if move[0] == turn]
        for i in now:
            give = add_block(ready, feed, i, sums, [arrived[m] for m, _ in FEEDS[i]],
                             [column for _, column in FEEDS[i]], BF)
            gives.append(give)
            back = tuple((target, source) for source, target in MOVES[i][2])
            arrived[i] = lax.ppermute(give, "batch", back)
        late = [arrived[i] for i in before]
        ready, small, *late = lax.optimization_barrier((row, small, *late, *gives))
        arrived.update(zip(before, late))
        before = now
        if steps:
            small = small + lax.ppermute(small, *steps.pop(0))
    for step in steps:
        small = small + lax.ppermute(small, *step)
    last = FEEDS[len(MOVES)]
    total = add_block(row, feed, len(MOVES), sums, [arrived[m] for m, _ in last],
                      [column for _, column in last], F32)
    return total, small


def slot_table(owners, capacity):
    panel_index = jnp.arange(owners.shape[0], dtype=jnp.int32)
    same_owner = (owners[:, None] == owners[None, :]) & (
        panel_index[None, :] < panel_index[:, None]
    )
    rank_within = jnp.sum(same_owner.astype(jnp.int32), axis=1)
    return owners * capacity + rank_within


def adam_update(weight, first_old, second_old, grad_now, step_count):
    step_float = step_count[0].astype(jnp.float32)
    first_new = beta_first * first_old + (1.0 - beta_first) * grad_now
    second_new = beta_second * second_old + (1.0 - beta_second) * grad_now * grad_now
    first_hat = first_new / (1.0 - jnp.power(beta_first, step_float))
    second_hat = second_new / (1.0 - jnp.power(beta_second, step_float))
    weight_new = weight - learn_rate * (
        first_hat / (jnp.sqrt(second_hat) + adam_eps) + decay_rate * weight
    )
    return (weight_new, first_new, second_new)


def local(
    tokens,
    grad_out,
    lengths,
    owners,
    weight_slots,
    first_slots,
    second_slots,
    small_params,
    small_first,
    small_second,
    step_count,
):
    capacity = weight_slots.shape[0]
    block_rows, features = tokens.shape[1:]
    slot_of = slot_table(owners, capacity)
    devices = lax.axis_size("seq") * lax.axis_size("batch")
    device = lax.axis_index("seq") * lax.axis_size("batch") + lax.axis_index("batch")
    limits = lengths - lax.axis_index("seq") * block_rows
    core = lax.axis_index("seq")
    batch = lax.axis_size("batch")
    half = batch * capacity
    owner_core = (owners >= batch).astype(jnp.int32)
    back = slot_of - owner_core * half + jnp.where(owner_core == core, 0, half)
    gathered = lax.all_gather(weight_slots.astype(BF), ("seq", "batch"), axis=0, tiled=True)
    q, k, v, ctx, probs, mixed, zh, rstd = attn_fwd(tokens, gathered, small_params, limits, slot_of)
    bias_hidden = small_params[8:].reshape(1, -1)
    layer_out, d_mixed, sums_ffn, d_bias, mine, theirs = ffn(
        mixed.reshape(-1, features), grad_out.reshape(-1, features), gathered, small_params,
        bias_hidden, slot_of, back, half)
    grad_in, sums_attn, mine, theirs = attn_bwd(
        d_mixed.reshape(tokens.shape), zh, rstd, tokens, q, k, v, ctx, probs, gathered,
        small_params, limits, slot_of, back, mine, theirs)
    small_local = jnp.concatenate(
        [sums_attn[0:2], sums_ffn[0:2], sums_attn[2:5], sums_ffn[2:3],
         d_bias.reshape(-1, features)], axis=0)
    if batch == 16 and lax.axis_size("seq") == 2:
        grad_slots, small_grad = reduce_slots(mine, theirs, small_local)
    else:
        both = jnp.where(core == 0, jnp.stack([mine, theirs]), jnp.stack([theirs, mine]))
        grad_slots = lax.psum_scatter(
            both.reshape((-1,) + mine.shape[1:]), ("seq", "batch"), scatter_dimension=0,
            tiled=True).astype(jnp.float32)
        small_grad = small_local
        for step in partners():
            small_grad = small_grad + lax.ppermute(small_grad, *step)
    held = jnp.sum((owners == device).astype(jnp.int32))
    used = jnp.arange(capacity, dtype=jnp.int32) < held
    grad_slots = jnp.where(used[:, None, None], grad_slots, 0.0)
    new_slots, new_first_slots, new_second_slots = adam_update(
        weight_slots, first_slots, second_slots, grad_slots, step_count
    )
    new_small, new_small_first, new_small_second = adam_update(
        small_params, small_first, small_second, small_grad, step_count
    )
    return (
        layer_out.reshape(tokens.shape),
        grad_in,
        grad_slots,
        new_slots,
        new_first_slots,
        new_second_slots,
        small_grad,
        new_small,
        new_small_first,
        new_small_second,
    )


def solution(mesh):
    in_specs = (
        P("batch", "seq", None),
        P("batch", "seq", None),
        P("batch"),
        P(),
        P(("seq", "batch"), None, None),
        P(("seq", "batch"), None, None),
        P(("seq", "batch"), None, None),
        P(),
        P(),
        P(),
        P(),
    )
    out_specs = (
        P("batch", "seq", None),
        P("batch", "seq", None),
        P(("seq", "batch"), None, None),
        P(("seq", "batch"), None, None),
        P(("seq", "batch"), None, None),
        P(("seq", "batch"), None, None),
        P(),
        P(),
        P(),
        P(),
    )
    return jax.shard_map(local, mesh=mesh, in_specs=in_specs, out_specs=out_specs, check_vma=False)
```
